32 devices in a mesh: clip: 2 (over y), row: 16 (over z, x, core).
Axes of the slice: x: 2, y: 2, z: 4, core: 2. Of those that a mesh axis runs over, the one named last changes fastest.
Arguments:
- features: bfloat16 [1, 64, 48, 384], P(None, ('clip', 'row')), parts along dimension 1, may hold values from -19 to 19
- conv_cache: bfloat16 [2, 64, 48, 384], P(None, ('clip', 'row')), parts along dimension 1, may hold values from -6 to 6
- norm_gain: float32 [384], replicated, may hold values from 0.1 to 1.9
- w_query: bfloat16 [384, 384], replicated
- w_key: bfloat16 [384, 384], replicated
- w_value: bfloat16 [384, 384], replicated, may hold values from -0.3125 to 0.3125
- w_out: bfloat16 [384, 384], replicated
- conv_gain: float32 [384], replicated, may hold values from 0.1 to 1.9
- conv_weight: bfloat16 [3, 3, 3, 384, 384], replicated, may hold values from -0.0625 to 0.0625
Outputs:
- residual_out: float32 [1, 64, 48, 384], P(None, ('clip', 'row')), parts along dimension 1
- conv_out: bfloat16 [1, 64, 48, 384], P(None, ('clip', 'row')), parts along dimension 1
The draws below stay inside these ranges and needn't reach their ends.
There are 2 independent parts, one for each index of `clip`. The reference program is written for one: setup_inputs(seed, part) draws one part's arguments, and reference() takes and returns one part's arrays. A program takes and returns all parts, laid end to end along the dimension named above; an argument that names none is the same for every part. Nothing has to cross between parts.
All inputs are finite; a program needn't handle non-finite values.
Results may differ from the reference program's by a relative error of at most 0.0096.
Values may be sent and summed in bfloat16 or wider, within the bound.
A program may use at most 128 MiB of HBM per device.

```python
import math
import jax
import jax.numpy as jnp
from jax import lax

C = 384
F = 1
W = 48
CACHE = 2
H = 32


def base_matrix(key):
    return jnp.clip(jax.random.normal(key, (C, C), jnp.float32), -6.0, 6.0) * C ** (-0.5)


def shared_query(key):
    matrix = base_matrix(jax.random.fold_in(key, 11))
    return matrix * 1.5


def draw_w_query(key, part):
    return shared_query(key).astype(jnp.bfloat16)


def draw_w_key(key, part):
    return (base_matrix(jax.random.fold_in(key, 12)) * 1.5).astype(jnp.bfloat16)


def draw_w_out(key, part):
    values = jnp.clip(jax.random.normal(jax.random.fold_in(key, 22), (C, C), jnp.float32), -6.0, 6.0)
    return (values * 8.0 * C ** (-0.5)).astype(jnp.bfloat16)


def draw_features(key, part):
    first_key = jax.random.fold_in(key, 31)
    noise = jnp.clip(jax.random.normal(first_key, (F, H, W, C), jnp.float32), -6.0, 6.0)
    return noise.astype(jnp.bfloat16)


def block_scale(key, dims, pieces, low, high):
    def one(position, blocks):
        draws = jax.random.uniform(jax.random.fold_in(jax.random.fold_in(key, 6), position), (blocks,), jnp.float32, low / len(pieces), high / len(pieces))
        return jnp.repeat(jnp.exp(draws), dims[position] // blocks).reshape((-1,) + (1,) * (len(dims) - position - 1))

    loudness = one(*pieces[0])
    for cut in pieces[1:]:
        loudness = loudness * one(*cut)
    return loudness


def centred(key, shape, width, bound, shards=(), kind=jnp.bfloat16):
    entries = jax.random.normal(key, shape, jnp.float32) * width
    if len(shards) > 0:
        entries = block_scale(key, shape, shards, -0.22, 0.18) * entries
    return jnp.clip(entries, min=-bound, max=bound).astype(kind)


def setup_inputs(seed: int = 0, part: int = 0) -> dict:
    splits = jax.random.split(jax.random.key(seed), 10)
    part_keys = jax.random.split(jax.random.fold_in(splits[9], part), 10)
    features = draw_features(jax.random.fold_in(jax.random.fold_in(splits[9], part), 71), part)
    conv_cache = centred(part_keys[1], (CACHE, H, W, C), 1.0, 6.0, ((1, 16),))
    norm_gain = jnp.clip(1.0 + 0.18 * jax.random.normal(splits[2], (C,), jnp.float32), 0.1, 1.9)
    w_query = draw_w_query(jax.random.fold_in(splits[9], 71), part)
    w_key = draw_w_key(jax.random.fold_in(splits[9], 71), part)
    w_value = centred(splits[5], (C, C), C ** -0.5, 0.3125)
    w_out = draw_w_out(jax.random.fold_in(splits[9], 71), part)
    conv_gain = jnp.clip(1.0 + 0.18 * jax.random.normal(splits[7], (C,), jnp.float32), 0.1, 1.9)
    conv_weight = centred(splits[8], (3, 3, 3, C, C), (27 * C) ** -0.5, 0.0625)
    return {"features": features, "conv_cache": conv_cache, "norm_gain": norm_gain, "w_query": w_query, "w_key": w_key, "w_value": w_value, "w_out": w_out, "conv_gain": conv_gain, "conv_weight": conv_weight}


def rms_norm(values, gain):
    return values * lax.rsqrt(lax.optimization_barrier(jnp.mean(values * values, axis=-1, keepdims=True)) + 1e-06) * gain

def reference(features, conv_cache, norm_gain, w_query, w_key, w_value, w_out, conv_gain, conv_weight):
    positions = H * W
    source = features.astype(jnp.float32)
    normed = rms_norm(source, norm_gain).astype(jnp.bfloat16).reshape(F * positions, C)

    def project(weight):
        return jnp.dot(normed, weight, preferred_element_type=jnp.float32).astype(jnp.bfloat16).reshape(F, positions, C)
    query = project(w_query)
    keyed = project(w_key)
    valued = project(w_value)
    block = math.gcd(positions, 512)
    score_scale = C ** (-0.5)

    def frame(operands):
        frame_query, frame_keys, frame_values = operands

        def attend(query_block):
            scores = jnp.dot(query_block, frame_keys.T, preferred_element_type=jnp.float32) * score_scale
            expw = jnp.exp(scores - lax.optimization_barrier(jnp.max(scores, axis=-1, keepdims=True)))
            total = lax.optimization_barrier(jnp.sum(expw, axis=-1, keepdims=True))
            summed = jnp.dot(expw.astype(jnp.bfloat16), frame_values, preferred_element_type=jnp.float32)
            return (summed / total).astype(jnp.bfloat16)
        return lax.map(attend, frame_query.reshape(positions // block, block, C)).reshape(positions, C)
    attended = lax.map(frame, (query, keyed, valued))
    residual_out = source + jnp.dot(attended.reshape(F * positions, C), w_out, preferred_element_type=jnp.float32).reshape(F, H, W, C)
    activated = jax.nn.silu(rms_norm(residual_out, conv_gain)).astype(jnp.bfloat16)
    extended = jnp.concatenate([conv_cache, activated], axis=0)
    padded = jnp.pad(extended, ((0, 0), (1, 1), (1, 1), (0, 0)))
    summed = jnp.zeros((F * positions, C), jnp.float32)
    for shift_t in range(3):
        for shift_y in range(3):
            for shift_x in range(3):
                window = padded[shift_t:shift_t + F, shift_y:shift_y + H, shift_x:shift_x + W].reshape(F * positions, C)
                summed = summed + jnp.dot(window, conv_weight[shift_t, shift_y, shift_x], preferred_element_type=jnp.float32)
    conv_out = summed.reshape(F, H, W, C).astype(jnp.bfloat16)
    return (residual_out, conv_out)
```

```python
import functools
import math

import jax
import jax.numpy as jnp
from jax import lax
from jax.experimental import pallas as pl
from jax.experimental.pallas import tpu as pltpu
from jax.sharding import PartitionSpec as P

MESH = pl.DeviceIdType.MESH
F32 = jnp.float32
BF16 = jnp.bfloat16
INNER = 4
UNROLL = 4
HALVES = 1
ORDER = (3, 1, 2)
DIRECT = {0: (1, 2, 3), 1: (0, 2), 2: (1, 0, 3), 3: (0, 2)}
RELAY = {0: ((3, 1),), 1: (), 2: ((1, 3),), 3: ()}
ARRIVE = {0: (1, 3, 2), 1: (0, 2, 3), 2: (1, 0, 3), 3: (2, 0, 1)}


def _rms(v, gain):
    return v * lax.rsqrt(jnp.mean(v * v, axis=-1, keepdims=True) + 1e-06) * gain


def _flip(index, bits):
    bit = 1
    while bit <= bits:
        if bits & bit:
            index = index + bit - 2 * bit * ((index // bit) % 2)
        bit *= 2
    return index


def _when(cond):
    if isinstance(cond, bool):
        return (lambda f: f()) if cond else (lambda f: None)
    return pl.when(cond)


def _both(a, b):
    if isinstance(a, bool) and isinstance(b, bool):
        return a and b
    return jnp.logical_and(a, b)


def ring(
    count,
    width,
    feat_hbm,
    cache_hbm,
    ng_hbm,
    wq_hbm,
    wk_hbm,
    wv_hbm,
    wo_hbm,
    cg_hbm,
    cw_hbm,
    res_ref,
    out_ref,
    ng_ref,
    cg_ref,
    blocks,
    src,
    ext,
    wq,
    wk,
    wv,
    wo,
    cw,
    qs,
    m_ref,
    l_ref,
    acc,
    cacc,
    load_sem,
    cw_sem,
    halo_send,
    halo_recv,
    z_send,
    x_send,
    c_send,
    recv,
):
    outer = count // INNER
    tokens, channels = feat_hbm.shape
    total = tokens + 2 * width
    me = lax.axis_index("row")
    z = me // INNER
    xpeer = me - z * INNER
    pair = (xpeer // 2) % 2
    core = xpeer % 2
    xpeer = me + 2 - 4 * pair
    cpeer = me + 1 - 2 * core
    static = outer == UNROLL
    piece = tokens // HALVES

    def zpeer(step):
        if static:
            return _flip(z, step)
        return lax.rem(z + step, outer)

    def zfrom(step):
        if static:
            return _flip(z, step)
        return lax.rem(z - step + outer, outer)

    def loop(low, high, body):
        if static:
            for step in range(low, high):
                body(step)
        else:
            lax.fori_loop(low, high, lambda i, carry: (body(i), carry)[1], 0)

    has_prev = me > 0
    has_next = me < count - 1
    prev = jnp.maximum(me - 1, 0)
    after = jnp.minimum(me + 1, count - 1)

    own = pl.ds(width, tokens)
    loads = [
        pltpu.make_async_copy(feat_hbm, src.at[own], load_sem.at[0]),
        pltpu.make_async_copy(wq_hbm, wq, load_sem.at[1]),
        pltpu.make_async_copy(wk_hbm, wk, load_sem.at[2]),
        pltpu.make_async_copy(cache_hbm, ext.at[:, own], load_sem.at[3]),
        pltpu.make_async_copy(wv_hbm, wv, load_sem.at[4]),
        pltpu.make_async_copy(wo_hbm, wo, load_sem.at[5]),
        pltpu.make_async_copy(cg_hbm, cg_ref, load_sem.at[6]),
    ]
    gains = pltpu.make_async_copy(ng_hbm, ng_ref, load_sem.at[7])
    gains.start()
    wloads = [pltpu.make_async_copy(cw_hbm.at[t], cw.at[t], cw_sem.at[t]) for t in range(3)]
    for copy in loads[:4]:
        copy.start()
    for copy in wloads[:2]:
        copy.start()
    for copy in loads[4:]:
        copy.start()
    wloads[2].start()

    barrier = pltpu.get_barrier_semaphore()

    def greet(device):
        pl.semaphore_signal(barrier, inc=1, device_id={"row": device}, device_id_type=MESH)

    def greet_z(step):
        greet(zpeer(step) * INNER + 2 * pair + core)

    loop(1, outer, greet_z)
    greet(xpeer)
    greet(cpeer)

    greet(lax.rem(me + 1, count))
    greet(lax.rem(me + count - 1, count))
    pl.semaphore_wait(barrier, outer + 3)

    def halo(a, b, index, device):
        return pltpu.make_async_remote_copy(
            src_ref=a,
            dst_ref=b,
            send_sem=halo_send.at[index],
            recv_sem=halo_recv.at[index],
            device_id={"row": device},
            device_id_type=MESH,
        )

    first = pl.ds(0, width)
    last = pl.ds(tokens - width, width)
    low = pl.ds(0, width)
    high = pl.ds(width + tokens, width)
    up_f = halo(feat_hbm.at[last], src.at[low], 0, after)
    down_f = halo(feat_hbm.at[first], src.at[high], 1, prev)
    up_c = halo(cache_hbm.at[:, last], ext.at[:, low], 2, after)
    down_c = halo(cache_hbm.at[:, first], ext.at[:, high], 3, prev)

    @pl.when(has_next)
    def _():
        up_f.start()

    @pl.when(has_prev)
    def _():
        down_f.start()

    def put(ident, h, sem, device):
        part = blocks.at[ident, pl.ds(h * piece, piece)]
        return pltpu.make_async_remote_copy(
            src_ref=part,
            dst_ref=part,
            send_sem=sem,
            recv_sem=recv.at[ident, h],
            device_id={"row": device},
            device_id_type=MESH,
        )

    def at(zi, p, c):
        return zi * INNER + 2 * p + c

    def z_put(step, h):
        if static and step == 2:
            return put(at(zpeer(3), pair, core), h, z_send.at[2, h], at(zpeer(1), pair, core))
        return put(me, h, z_send.at[step, h], at(zpeer(step), pair, core))

    def x_put(step, h):
        return put(at(zfrom(step), pair, core), h, x_send.at[step, h], xpeer)

    def c_put(step, h, which):
        p = pair if which == 0 else 1 - pair
        return put(at(zfrom(step), p, core), h, c_send.at[which, step, h], cpeer)

    def arrived(ident, h):
        put(ident, h, z_send.at[0, h], cpeer).wait_recv()

    gains.wait()
    gain = ng_ref[...].reshape(1, channels)
    loads[0].wait()
    blocks[me] = _rms(src[own, :].astype(F32), gain).astype(BF16)
    opening = [s for s in ORDER if s != 2] if static else range(1, min(outer, 3))
    for s in opening:
        for h in range(HALVES):
            if s == opening[0] or not static:
                z_put(s, h).start()
            if s == opening[0]:
                x_put(0, h).start()
    for h in range(HALVES):
        c_put(0, h, 0).start()

    @pl.when(has_next)
    def _():
        up_c.start()

    @pl.when(has_prev)
    def _():
        down_c.start()

    zero = jnp.zeros((width, channels), BF16)

    @pl.when(has_prev)
    def _():
        up_f.wait_recv()

    @pl.when(jnp.logical_not(has_prev))
    def _():
        src[low, :] = zero
        for t in range(ext.shape[0]):
            ext[t, low, :] = zero

    @pl.when(has_next)
    def _():
        down_f.wait_recv()

    @pl.when(jnp.logical_not(has_next))
    def _():
        src[high, :] = zero
        for t in range(ext.shape[0]):
            ext[t, high, :] = zero

    if static:
        z_put(opening[0], 0).wait_send()
        z_put(opening[1], 0).start()
    loads[1].wait()
    loads[2].wait()
    normed = _rms(src[...].astype(F32), gain).astype(BF16)
    query = jnp.dot(normed, wq[...], preferred_element_type=F32).astype(BF16)
    folded = lax.dot_general(
        query, wk[...], (((1,), (1,)), ((), ())), preferred_element_type=F32
    )
    qs[...] = (folded * (channels**-0.5 * math.log2(math.e))).astype(BF16)
    m_ref[...] = jnp.full(m_ref.shape, -1e30, F32)
    l_ref[...] = jnp.zeros(l_ref.shape, F32)
    acc[...] = jnp.zeros(acc.shape, F32)

    def conv(frame, t):
        taps = jnp.concatenate(
            [frame[dy * width : dy * width + tokens] for dy in range(3)], axis=-1
        )
        for dx in range(3):
            part = jnp.dot(
                taps,
                cw[t, :, dx].reshape(3 * channels, channels),
                preferred_element_type=F32,
            )
            if t == 0:
                cacc[dx] = part
            else:
                cacc[dx] += part

    def attend(step):
        zi = zfrom(step)
        keys = blocks[pl.ds(zi * INNER, INNER)].reshape(INNER * tokens, channels)
        scores = lax.dot_general(
            qs[...], keys, (((1,), (1,)), ((), ())), preferred_element_type=F32
        )
        old = m_ref[...]
        new = jnp.maximum(old, jnp.max(scores, axis=-1, keepdims=True))
        scale = jnp.exp2(old - new)
        expw = jnp.exp2(scores - new)
        m_ref[...] = new
        l_ref[...] = l_ref[...] * scale + jnp.sum(expw, axis=-1, keepdims=True)
        acc[...] = acc[...] * scale + jnp.dot(
            expw.astype(BF16), keys, preferred_element_type=F32
        )

    def stage_z(step, h):
        if not static:
            z_put(step, h).wait_send()

            @pl.when(step + 2 < outer)
            def _():
                z_put(step + 2, h).start()

        arrived(at(zfrom(step), pair, core), h)
        if static and step == 3:
            z_put(2, h).start()
        x_put(step, h).start()
        c_put(step, h, 0).start()

    def stage_x(step, h):
        arrived(at(zfrom(step), 1 - pair, core), h)
        c_put(step, h, 1).start()

    def stage_c(step, h):
        zi = zfrom(step)
        arrived(at(zi, pair, 1 - core), h)
        arrived(at(zi, 1 - pair, 1 - core), h)
        if h == HALVES - 1:
            attend(step)

    loads[3].wait()

    @pl.when(has_prev)
    def _():
        up_c.wait_recv()

    @pl.when(has_next)
    def _():
        down_c.wait_recv()

    if static:
        zunits = [(s, h) for s in ORDER for h in range(HALVES)]
        units = [(0, h) for h in range(HALVES)] + zunits
        for i in range(len(units) + 1):
            if i < len(zunits):
                stage_z(*zunits[i])
            if i < len(units):
                stage_x(*units[i])
            if i < 2:
                wloads[i].wait()
                conv(ext[i], i)
            if i > 0:
                stage_c(*units[i - 1])
    else:
        pieces = range(HALVES)
        for t in range(2):
            wloads[t].wait()
            conv(ext[t], t)
        for h in pieces:
            stage_x(0, h)
        for h in pieces:
            stage_z(1, h)

        def body(step):
            for h in pieces:
                stage_z(step, h)
            for h in pieces:
                stage_x(step - 1, h)
            for h in pieces:
                stage_c(step - 2, h)

        loop(2, outer, body)
        for h in pieces:
            stage_x(outer - 1, h)
        for s in (outer - 2, outer - 1):
            for h in pieces:
                stage_c(s, h)

    loads[4].wait()
    loads[5].wait()
    loads[6].wait()
    mixed = (acc[...] / l_ref[...]).astype(BF16)
    attended = jnp.dot(mixed, wv[...], preferred_element_type=F32).astype(BF16)
    residual = src[...].astype(F32) + jnp.dot(attended, wo[...], preferred_element_type=F32)
    res_ref[...] = residual[width : width + tokens]
    v = _rms(residual, cg_ref[...].reshape(1, channels))
    activated = v / (1.0 + jnp.exp(-v))
    spot = lax.broadcasted_iota(jnp.int32, (total, 1), 0)
    start = jnp.where(has_prev, 0, width)
    stop = jnp.where(has_next, total, total - width)
    activated = jnp.where((spot >= start) & (spot < stop), activated, 0.0).astype(BF16)
    wloads[2].wait()
    conv(activated, 2)
    column = lax.broadcasted_iota(jnp.int32, (tokens, 1), 0) % width
    left = jnp.where(column == 0, 0.0, pltpu.roll(cacc[0], 1, 0))
    right = jnp.where(column == width - 1, 0.0, pltpu.roll(cacc[2], tokens - 1, 0))
    out_ref[...] = (left + cacc[1] + right).astype(BF16)

    for h in range(HALVES):
        if static:
            for s in (opening[1], 2):
                z_put(s, h).wait_send()
        loop(0, outer, lambda s: x_put(s, h).wait_send())
        loop(0, outer, lambda s: c_put(s, h, 0).wait_send())
        loop(0, outer, lambda s: c_put(s, h, 1).wait_send())

    @pl.when(has_next)
    def _():
        up_f.wait_send()
        up_c.wait_send()

    @pl.when(has_prev)
    def _():
        down_f.wait_send()
        down_c.wait_send()


def among(z, values):
    if all(v == values[0] for v in values):
        return values[0]
    out = values[-1]
    for i in range(len(values) - 1):
        out = jnp.where(z == i, values[i], out)
    return out


def column_plan():
    flips = {}
    for z in range(UNROLL):
        for q in range(UNROLL):
            relayed = any((q, z) in RELAY[a] for a in range(UNROLL))
            flips[z, q] = 0 if relayed else 1
    sends = {(a, b) for a in range(UNROLL) for b in DIRECT[a]}
    sends |= {(a, d) for a in range(UNROLL) for _, d in RELAY[a]}
    return flips, sends


def grid_kernel(
    count,
    width,
    feat_hbm,
    cache_hbm,
    ng_hbm,
    wq_hbm,
    wk_hbm,
    wv_hbm,
    wo_hbm,
    cg_hbm,
    cw_hbm,
    res_ref,
    out_ref,
    ng_ref,
    cg_ref,
    blocks,
    src,
    ext,
    wq,
    wk,
    wv,
    wo,
    wvo,
    cw,
    qs,
    m_ref,
    l_ref,
    acc,
    part_acc,
    part_ml,
    peer_acc,
    peer_ml,
    cacc,
    load_sem,
    cw_sem,
    halo_send,
    halo_recv,
    own_send,
    relay_send,
    x_send,
    recv,
    pair_send,
    pair_recv,
    reply,
):
    tokens, channels = feat_hbm.shape
    total = tokens + 2 * width
    half = tokens + width
    me = lax.axis_index("row")
    z = me // INNER
    x = (me // 2) % 2
    c = me % 2
    flips, sends = column_plan()
    planes = range(UNROLL)

    def at(zi, xi, ci):
        return zi * INNER + 2 * xi + ci

    xpeer = at(z, 1 - x, 1 - c)
    cpeer = at(z, x, 1 - c)
    has_prev = me > 0
    has_next = me < count - 1
    prev = jnp.maximum(me - 1, 0)
    after = jnp.minimum(me + 1, count - 1)
    down_plane = (x == 0) & (c == 0) & (z > 0)
    up_plane = (x == 1) & (c == 1) & (z < UNROLL - 1)

    def flagged(values):
        chosen = among(z, [int(v) for v in values])
        return bool(chosen) if isinstance(chosen, int) else chosen == 1

    def signal(sem, device):
        pl.semaphore_signal(sem, inc=1, device_id={"row": device}, device_id_type=MESH)

    def partners(a, b):
        return (a, b) in sends or (b, a) in sends

    barrier = pltpu.get_barrier_semaphore()
    for q in planes:
        @_when(flagged([q > a and partners(a, q) for a in planes]))
        def _():
            signal(barrier, at(q, x, 1 - c))

    @pl.when(x == 0)
    def _():
        signal(barrier, xpeer)

    @pl.when(c == 0)
    def _():
        signal(barrier, cpeer)

    @pl.when(up_plane)
    def _():
        signal(barrier, after)

    own = pl.ds(width, tokens)
    loads = [
        pltpu.make_async_copy(feat_hbm, src.at[own], load_sem.at[0]),
        pltpu.make_async_copy(wq_hbm, wq, load_sem.at[1]),
        pltpu.make_async_copy(wk_hbm, wk, load_sem.at[2]),
        pltpu.make_async_copy(cache_hbm, ext.at[:, own], load_sem.at[3]),
        pltpu.make_async_copy(wv_hbm, wv, load_sem.at[4]),
        pltpu.make_async_copy(wo_hbm, wo, load_sem.at[5]),
        pltpu.make_async_copy(cg_hbm, cg_ref, load_sem.at[6]),
        pltpu.make_async_copy(ng_hbm, ng_ref, load_sem.at[7]),
    ]
    wloads = [pltpu.make_async_copy(cw_hbm.at[t], cw.at[t], cw_sem.at[t]) for t in range(3)]
    loads[0].start()
    loads[7].start()

    lower = among(z, [sum(partners(q, a) for q in range(a)) for a in planes])

    @pl.when(me > 0)
    def _():
        pl.semaphore_wait(barrier, lower + x + c + jnp.where(down_plane, 1, 0))

    for q in planes[:-1]:
        @_when(flagged([q < a and (q, a) in sends for a in planes]))
        def _():
            signal(reply.at[z], at(q, x, 1 - c))

    @pl.when(x == 1)
    def _():
        signal(reply.at[UNROLL], xpeer)

    @pl.when(c == 1)
    def _():
        signal(reply.at[UNROLL + 1], cpeer)

    @pl.when(down_plane)
    def _():
        signal(reply.at[UNROLL + 2], prev)

    for copy in (loads[1], loads[2], loads[4], loads[5], loads[3], wloads[0], wloads[1], loads[6], wloads[2]):
        copy.start()

    def remote(a, b, send, receive, device):
        return pltpu.make_async_remote_copy(
            src_ref=a,
            dst_ref=b,
            send_sem=send,
            recv_sem=receive,
            device_id={"row": device},
            device_id_type=MESH,
        )

    def halo(a, b, index, device):
        return remote(a, b, halo_send.at[index], halo_recv.at[index], device)

    first = pl.ds(0, width)
    last = pl.ds(tokens - width, width)
    low = pl.ds(0, width)
    high = pl.ds(width + tokens, width)
    up_f = halo(feat_hbm.at[last], src.at[low], 0, after)
    down_f = halo(feat_hbm.at[first], src.at[high], 1, prev)
    up_c = halo(cache_hbm.at[:, last], ext.at[:, low], 2, after)
    down_c = halo(cache_hbm.at[:, first], ext.at[:, high], 3, prev)

    def put(ident, device, sem):
        part = blocks.at[ident]
        return remote(part, part, sem, recv.at[ident], device)

    def z_send(j):
        dest = among(z, [DIRECT[a][j] if j < len(DIRECT[a]) else 0 for a in planes])

        @_when(flagged([j < len(DIRECT[a]) for a in planes]))
        def _():
            @pl.when(dest > z)
            def _():
                pl.semaphore_wait(reply.at[dest], 1)

            put(me, at(dest, x, 1 - c), own_send.at[j]).start()

    def x_own():
        @pl.when(x == 0)
        def _():
            pl.semaphore_wait(reply.at[UNROLL], 1)

        put(me, xpeer, own_send.at[3]).start()

    def arrived(ident):
        put(ident, cpeer, own_send.at[0]).wait_recv()

    loads[0].wait()
    loads[7].wait()
    gain = ng_ref[...].reshape(1, channels)
    blocks[me] = _rms(src[own, :].astype(F32), gain).astype(BF16)
    z_send(0)
    z_send(1)
    x_own()

    @pl.when(c == 0)
    def _():
        pl.semaphore_wait(reply.at[UNROLL + 1], 1)

    @pl.when(up_plane)
    def _():
        pl.semaphore_wait(reply.at[UNROLL + 2], 1)

    @pl.when(has_next)
    def _():
        up_f.start()
        up_c.start()

    @pl.when(has_prev)
    def _():
        down_f.start()
        down_c.start()

    z_send(2)

    zero = jnp.zeros((width, channels), BF16)

    @pl.when(jnp.logical_not(has_prev))
    def _():
        src[low, :] = zero
        for t in range(ext.shape[0]):
            ext[t, low, :] = zero

    @pl.when(jnp.logical_not(has_next))
    def _():
        src[high, :] = zero
        for t in range(ext.shape[0]):
            ext[t, high, :] = zero

    def conv(frame, t):
        taps = jnp.concatenate(
            [frame[dy * width : dy * width + tokens] for dy in range(3)], axis=-1
        )
        for dx in range(3):
            part = jnp.dot(
                taps,
                cw[t, :, dx].reshape(3 * channels, channels),
                preferred_element_type=F32,
            )
            if t == 0:
                cacc[dx] = part
            else:
                cacc[dx] += part

    def attend(idents, opening=False):
        keys = jnp.concatenate([blocks[u] for u in idents], axis=0)
        scores = lax.dot_general(
            qs[...], keys, (((1,), (1,)), ((), ())), preferred_element_type=F32
        )
        peak = jnp.max(scores, axis=-1, keepdims=True)
        if opening:
            new = peak
        else:
            old = m_ref[...]
            new = jnp.maximum(old, peak)
            scale = jnp.exp2(old - new)
        expw = jnp.exp2(scores - new)
        m_ref[...] = new
        mass = jnp.sum(expw, axis=-1, keepdims=True)
        value = jnp.dot(expw.astype(BF16), keys, preferred_element_type=F32)
        if opening:
            l_ref[...] = mass
            acc[...] = value
        else:
            l_ref[...] = l_ref[...] * scale + mass
            acc[...] = acc[...] * scale + value

    def column(j):
        q = among(z, [ARRIVE[a][j] for a in planes])
        flip = among(z, [flips[a, ARRIVE[a][j]] for a in planes])
        return q, c + flip - 2 * c * flip

    def stage_z(j):
        q, core = column(j)
        ident = at(q, x, core)
        arrived(ident)
        if any(RELAY.values()):
            relayed = among(z, [RELAY[a][0][0] if RELAY[a] else UNROLL for a in planes])
            dest = among(z, [RELAY[a][0][1] if RELAY[a] else 0 for a in planes])

            @pl.when(q == relayed)
            def _():
                put(ident, at(dest, x, 1 - c), relay_send.at[0]).start()

        put(ident, xpeer, x_send.at[j]).start()
        return ident

    def stage_x(j):
        q, core = column(j)
        ident = at(q, 1 - x, 1 - core)
        arrived(ident)
        return ident

    loads[4].wait()
    loads[5].wait()
    wvo[...] = jnp.dot(wv[...], wo[...], preferred_element_type=F32).astype(BF16)

    z0 = stage_z(0)

    @pl.when(has_prev)
    def _():
        up_f.wait_recv()

    @pl.when(has_next)
    def _():
        down_f.wait_recv()

    loads[1].wait()
    loads[2].wait()
    mine = pl.ds(pl.multiple_of(c * half, 16), half)
    rows = src[pl.ds(pl.multiple_of(c * width, 16), half), :].astype(F32)
    query = jnp.dot(_rms(rows, gain).astype(BF16), wq[...], preferred_element_type=F32).astype(BF16)
    folded = lax.dot_general(
        query, wk[...], (((1,), (1,)), ((), ())), preferred_element_type=F32
    )
    qs[mine, :] = (folded * (channels**-0.5 * math.log2(math.e))).astype(BF16)
    share = remote(qs.at[mine], qs.at[mine], pair_send.at[0], pair_recv.at[0], cpeer)
    share.start()

    z1 = stage_z(1)
    arrived(xpeer)
    share.wait_recv()
    attend([me, xpeer], True)
    z2 = stage_z(2)
    attend([z0, z1])

    loads[3].wait()

    @pl.when(has_prev)
    def _():
        up_c.wait_recv()

    @pl.when(has_next)
    def _():
        down_c.wait_recv()

    for t in range(2):
        wloads[t].wait()
        conv(ext[t], t)

    x0 = stage_x(0)
    attend([z2, x0])
    x1 = stage_x(1)
    x2 = stage_x(2)
    attend([x1, x2])

    theirs = pl.ds(pl.multiple_of((1 - c) * tokens, 16), total)
    window = pl.ds(pl.multiple_of(c * tokens, 16), total)
    part_acc[...] = acc[theirs, :].astype(BF16)
    lane = lax.broadcasted_iota(jnp.int32, part_ml.shape, 1)
    part_ml[...] = jnp.where(lane < part_ml.shape[1] // 2, m_ref[theirs, :], l_ref[theirs, :])
    give = [
        remote(part_acc, peer_acc, pair_send.at[1], pair_recv.at[1], cpeer),
        remote(part_ml, peer_ml, pair_send.at[2], pair_recv.at[2], cpeer),
    ]
    for copy in give:
        copy.start()

    for j in range(3):
        @_when(flagged([j < len(DIRECT[a]) for a in planes]))
        def _():
            put(me, cpeer, own_send.at[j]).wait_send()

        put(me, cpeer, x_send.at[j]).wait_send()
    put(me, cpeer, own_send.at[3]).wait_send()

    @_when(flagged([bool(RELAY[a]) for a in planes]))
    def _():
        put(me, cpeer, relay_send.at[0]).wait_send()

    @pl.when(has_next)
    def _():
        up_f.wait_send()
        up_c.wait_send()

    @pl.when(has_prev)
    def _():
        down_f.wait_send()
        down_c.wait_send()

    share.wait_send()
    loads[6].wait()
    wloads[2].wait()
    for copy in give:
        copy.wait()

    peer_m = peer_ml[:, :1]
    peer_l = peer_ml[:, part_ml.shape[1] // 2 :][:, :1]
    own_m = m_ref[window, :]
    new = jnp.maximum(own_m, peer_m)
    own_w = jnp.exp2(own_m - new)
    peer_w = jnp.exp2(peer_m - new)
    inverse = 1.0 / (l_ref[window, :] * own_w + peer_l * peer_w)
    mixed = acc[window, :] * (own_w * inverse) + peer_acc[...].astype(F32) * (peer_w * inverse)
    residual = src[...].astype(F32) + jnp.dot(
        mixed.astype(BF16), wvo[...], preferred_element_type=F32
    )
    res_ref[...] = residual[width : width + tokens]
    v = _rms(residual, cg_ref[...].reshape(1, channels))
    activated = v / (1.0 + jnp.exp(-v))
    spot = lax.broadcasted_iota(jnp.int32, (total, 1), 0)
    start = jnp.where(has_prev, 0, width)
    stop = jnp.where(has_next, total, total - width)
    activated = jnp.where((spot >= start) & (spot < stop), activated, 0.0).astype(BF16)
    conv(activated, 2)
    column_of = lax.broadcasted_iota(jnp.int32, (tokens, 1), 0) % width
    left = jnp.where(column_of == 0, 0.0, pltpu.roll(cacc[0], 1, 0))
    right = jnp.where(column_of == width - 1, 0.0, pltpu.roll(cacc[2], tokens - 1, 0))
    out_ref[...] = (left + cacc[1] + right).astype(BF16)


def shards(features, conv_cache, norm_gain, w_query, w_key, w_value, w_out, conv_gain, conv_weight):
    frames, rows, width, channels = features.shape
    cached = conv_cache.shape[0]
    tokens = rows * width
    total = tokens + 2 * width
    count = lax.axis_size("row")
    outer = count // INNER
    hbm = pl.BlockSpec(memory_space=pltpu.HBM)
    vmem = pl.BlockSpec(memory_space=pltpu.VMEM)
    dma = pltpu.SemaphoreType.DMA
    square = pltpu.VMEM((channels, channels), BF16)
    lead = [pltpu.VMEM((channels,), F32), pltpu.VMEM((channels,), F32), pltpu.VMEM((count, tokens, channels), BF16)]
    lead += [pltpu.VMEM((total, channels), BF16), pltpu.VMEM((cached, total, channels), BF16)]
    lead += [square, square, square, square]
    kernels = pltpu.VMEM(conv_weight.shape, BF16)
    summed = pltpu.VMEM((3, tokens, channels), F32)
    if outer == UNROLL:
        body = grid_kernel
        both = 2 * (tokens + width)
        lanes = 128
        scratch = lead + [
            square,
            kernels,
            pltpu.VMEM((both, channels), BF16),
            pltpu.VMEM((both, 1), F32),
            pltpu.VMEM((both, 1), F32),
            pltpu.VMEM((both, channels), F32),
            pltpu.VMEM((total, channels), BF16),
            pltpu.VMEM((total, lanes), F32),
            pltpu.VMEM((total, channels), BF16),
            pltpu.VMEM((total, lanes), F32),
            summed,
            dma((8,)),
            dma((3,)),
            dma((4,)),
            dma((4,)),
            dma((4,)),
            dma((1,)),
            dma((3,)),
            dma((count,)),
            dma((3,)),
            dma((3,)),
            pltpu.SemaphoreType.REGULAR((UNROLL + 3,)),
        ]
    else:
        body = ring
        scratch = lead + [
            kernels,
            pltpu.VMEM((total, channels), BF16),
            pltpu.VMEM((total, 1), F32),
            pltpu.VMEM((total, 1), F32),
            pltpu.VMEM((total, channels), F32),
            summed,
            dma((8,)),
            dma((3,)),
            dma((4,)),
            dma((4,)),
            dma((outer, HALVES)),
            dma((outer, HALVES)),
            dma((2, outer, HALVES)),
            dma((count, HALVES)),
        ]
    residual, conv_out = pl.pallas_call(
        functools.partial(body, count, width),
        out_shape=(
            jax.ShapeDtypeStruct((tokens, channels), F32),
            jax.ShapeDtypeStruct((tokens, channels), BF16),
        ),
        in_specs=[hbm] * 9,
        out_specs=(vmem, vmem),
        scratch_shapes=scratch,
        compiler_params=pltpu.CompilerParams(
            collective_id=0, has_side_effects=True, vmem_limit_bytes=48 << 20
        ),
    )(
        *(
            pltpu.with_memory_space_constraint(x, pltpu.HBM)
            for x in (
                features.reshape(tokens, channels),
                conv_cache.reshape(cached, tokens, channels),
                norm_gain,
                w_query,
                w_key,
                w_value,
                w_out,
                conv_gain,
                conv_weight,
            )
        )
    )
    return (
        residual.reshape(frames, rows, width, channels),
        conv_out.reshape(frames, rows, width, channels),
    )


def solution(mesh):
    placed = (
        P(None, ("clip", "row"), None, None),
        P(None, ("clip", "row"), None, None),
        P(),
        P(),
        P(),
        P(),
        P(),
        P(),
        P(),
    )
    return jax.shard_map(
        shards,
        mesh=mesh,
        in_specs=placed,
        out_specs=(P(None, ("clip", "row"), None, None), P(None, ("clip", "row"), None, None)),
        check_vma=False,
    )
```

```python
import functools
import math

import jax
import jax.numpy as jnp
from jax import lax
from jax.experimental import pallas as pl
from jax.experimental.pallas import tpu as pltpu
from jax.sharding import PartitionSpec as P

MESH = pl.DeviceIdType.MESH
F32 = jnp.float32
BF16 = jnp.bfloat16
INNER = 4
UNROLL = 4
HALVES = 1
ORDER = (3, 1, 2)
DIRECT = {0: (1, 2, 3), 1: (0, 2), 2: (1, 0, 3), 3: (0, 2)}
RELAY = {0: ((3, 1),), 1: (), 2: ((1, 3),), 3: ()}
ARRIVE = {0: (1, 3, 2), 1: (0, 2, 3), 2: (1, 0, 3), 3: (2, 0, 1)}


def _rms(v, gain):
    return v * lax.rsqrt(jnp.mean(v * v, axis=-1, keepdims=True) + 1e-06) * gain


def _flip(index, bits):
    bit = 1
    while bit <= bits:
        if bits & bit:
            index = index + bit - 2 * bit * ((index // bit) % 2)
        bit *= 2
    return index


def _when(cond):
    if isinstance(cond, bool):
        return (lambda f: f()) if cond else (lambda f: None)
    return pl.when(cond)


def _both(a, b):
    if isinstance(a, bool) and isinstance(b, bool):
        return a and b
    return jnp.logical_and(a, b)


def ring(
    count,
    width,
    feat_hbm,
    cache_hbm,
    ng_hbm,
    wq_hbm,
    wk_hbm,
    wv_hbm,
    wo_hbm,
    cg_hbm,
    cw_hbm,
    res_ref,
    out_ref,
    ng_ref,
    cg_ref,
    blocks,
    src,
    ext,
    wq,
    wk,
    wv,
    wo,
    cw,
    qs,
    m_ref,
    l_ref,
    acc,
    cacc,
    load_sem,
    cw_sem,
    halo_send,
    halo_recv,
    z_send,
    x_send,
    c_send,
    recv,
):
    outer = count // INNER
    tokens, channels = feat_hbm.shape
    total = tokens + 2 * width
    me = lax.axis_index("row")
    z = me // INNER
    xpeer = me - z * INNER
    pair = (xpeer // 2) % 2
    core = xpeer % 2
    xpeer = me + 2 - 4 * pair
    cpeer = me + 1 - 2 * core
    static = outer == UNROLL
    piece = tokens // HALVES

    def zpeer(step):
        if static:
            return _flip(z, step)
        return lax.rem(z + step, outer)

    def zfrom(step):
        if static:
            return _flip(z, step)
        return lax.rem(z - step + outer, outer)

    def loop(low, high, body):
        if static:
            for step in range(low, high):
                body(step)
        else:
            lax.fori_loop(low, high, lambda i, carry: (body(i), carry)[1], 0)

    has_prev = me > 0
    has_next = me < count - 1
    prev = jnp.maximum(me - 1, 0)
    after = jnp.minimum(me + 1, count - 1)

    own = pl.ds(width, tokens)
    loads = [
        pltpu.make_async_copy(feat_hbm, src.at[own], load_sem.at[0]),
        pltpu.make_async_copy(wq_hbm, wq, load_sem.at[1]),
        pltpu.make_async_copy(wk_hbm, wk, load_sem.at[2]),
        pltpu.make_async_copy(cache_hbm, ext.at[:, own], load_sem.at[3]),
        pltpu.make_async_copy(wv_hbm, wv, load_sem.at[4]),
        pltpu.make_async_copy(wo_hbm, wo, load_sem.at[5]),
        pltpu.make_async_copy(cg_hbm, cg_ref, load_sem.at[6]),
    ]
    gains = pltpu.make_async_copy(ng_hbm, ng_ref, load_sem.at[7])
    gains.start()
    wloads = [pltpu.make_async_copy(cw_hbm.at[t], cw.at[t], cw_sem.at[t]) for t in range(3)]
    for copy in loads[:4]:
        copy.start()
    for copy in wloads[:2]:
        copy.start()
    for copy in loads[4:]:
        copy.start()
    wloads[2].start()

    barrier = pltpu.get_barrier_semaphore()

    def greet(device):
        pl.semaphore_signal(barrier, inc=1, device_id={"row": device}, device_id_type=MESH)

    def greet_z(step):
        greet(zpeer(step) * INNER + 2 * pair + core)

    loop(1, outer, greet_z)
    greet(xpeer)
    greet(cpeer)

    greet(lax.rem(me + 1, count))
    greet(lax.rem(me + count - 1, count))
    pl.semaphore_wait(barrier, outer + 3)

    def halo(a, b, index, device):
        return pltpu.make_async_remote_copy(
            src_ref=a,
            dst_ref=b,
            send_sem=halo_send.at[index],
            recv_sem=halo_recv.at[index],
            device_id={"row": device},
            device_id_type=MESH,
        )

    first = pl.ds(0, width)
    last = pl.ds(tokens - width, width)
    low = pl.ds(0, width)
    high = pl.ds(width + tokens, width)
    up_f = halo(feat_hbm.at[last], src.at[low], 0, after)
    down_f = halo(feat_hbm.at[first], src.at[high], 1, prev)
    up_c = halo(cache_hbm.at[:, last], ext.at[:, low], 2, after)
    down_c = halo(cache_hbm.at[:, first], ext.at[:, high], 3, prev)

    @pl.when(has_next)
    def _():
        up_f.start()

    @pl.when(has_prev)
    def _():
        down_f.start()

    def put(ident, h, sem, device):
        part = blocks.at[ident, pl.ds(h * piece, piece)]
        return pltpu.make_async_remote_copy(
            src_ref=part,
            dst_ref=part,
            send_sem=sem,
            recv_sem=recv.at[ident, h],
            device_id={"row": device},
            device_id_type=MESH,
        )

    def at(zi, p, c):
        return zi * INNER + 2 * p + c

    def z_put(step, h):
        if static and step == 2:
            return put(at(zpeer(3), pair, core), h, z_send.at[2, h], at(zpeer(1), pair, core))
        return put(me, h, z_send.at[step, h], at(zpeer(step), pair, core))

    def x_put(step, h):
        return put(at(zfrom(step), pair, core), h, x_send.at[step, h], xpeer)

    def c_put(step, h, which):
        p = pair if which == 0 else 1 - pair
        return put(at(zfrom(step), p, core), h, c_send.at[which, step, h], cpeer)

    def arrived(ident, h):
        put(ident, h, z_send.at[0, h], cpeer).wait_recv()

    gains.wait()
    gain = ng_ref[...].reshape(1, channels)
    loads[0].wait()
    blocks[me] = _rms(src[own, :].astype(F32), gain).astype(BF16)
    opening = [s for s in ORDER if s != 2] if static else range(1, min(outer, 3))
    for s in opening:
        for h in range(HALVES):
            if s == opening[0] or not static:
                z_put(s, h).start()
            if s == opening[0]:
                x_put(0, h).start()
    for h in range(HALVES):
        c_put(0, h, 0).start()

    @pl.when(has_next)
    def _():
        up_c.start()

    @pl.when(has_prev)
    def _():
        down_c.start()

    zero = jnp.zeros((width, channels), BF16)

    @pl.when(has_prev)
    def _():
        up_f.wait_recv()

    @pl.when(jnp.logical_not(has_prev))
    def _():
        src[low, :] = zero
        for t in range(ext.shape[0]):
            ext[t, low, :] = zero

    @pl.when(has_next)
    def _():
        down_f.wait_recv()

    @pl.when(jnp.logical_not(has_next))
    def _():
        src[high, :] = zero
        for t in range(ext.shape[0]):
            ext[t, high, :] = zero

    if static:
        z_put(opening[0], 0).wait_send()
        z_put(opening[1], 0).start()
    loads[1].wait()
    loads[2].wait()
    normed = _rms(src[...].astype(F32), gain).astype(BF16)
    query = jnp.dot(normed, wq[...], preferred_element_type=F32).astype(BF16)
    folded = lax.dot_general(
        query, wk[...], (((1,), (1,)), ((), ())), preferred_element_type=F32
    )
    qs[...] = (folded * (channels**-0.5 * math.log2(math.e))).astype(BF16)
    m_ref[...] = jnp.full(m_ref.shape, -1e30, F32)
    l_ref[...] = jnp.zeros(l_ref.shape, F32)
    acc[...] = jnp.zeros(acc.shape, F32)

    def conv(frame, t):
        taps = jnp.concatenate(
            [frame[dy * width : dy * width + tokens] for dy in range(3)], axis=-1
        )
        for dx in range(3):
            part = jnp.dot(
                taps,
                cw[t, :, dx].reshape(3 * channels, channels),
                preferred_element_type=F32,
            )
            if t == 0:
                cacc[dx] = part
            else:
                cacc[dx] += part

    def attend(step):
        zi = zfrom(step)
        keys = blocks[pl.ds(zi * INNER, INNER)].reshape(INNER * tokens, channels)
        scores = lax.dot_general(
            qs[...], keys, (((1,), (1,)), ((), ())), preferred_element_type=F32
        )
        old = m_ref[...]
        new = jnp.maximum(old, jnp.max(scores, axis=-1, keepdims=True))
        scale = jnp.exp2(old - new)
        expw = jnp.exp2(scores - new)
        m_ref[...] = new
        l_ref[...] = l_ref[...] * scale + jnp.sum(expw, axis=-1, keepdims=True)
        acc[...] = acc[...] * scale + jnp.dot(
            expw.astype(BF16), keys, preferred_element_type=F32
        )

    def stage_z(step, h):
        if not static:
            z_put(step, h).wait_send()

            @pl.when(step + 2 < outer)
            def _():
                z_put(step + 2, h).start()

        arrived(at(zfrom(step), pair, core), h)
        if static and step == 3:
            z_put(2, h).start()
        x_put(step, h).start()
        c_put(step, h, 0).start()

    def stage_x(step, h):
        arrived(at(zfrom(step), 1 - pair, core), h)
        c_put(step, h, 1).start()

    def stage_c(step, h):
        zi = zfrom(step)
        arrived(at(zi, pair, 1 - core), h)
        arrived(at(zi, 1 - pair, 1 - core), h)
        if h == HALVES - 1:
            attend(step)

    loads[3].wait()

    @pl.when(has_prev)
    def _():
        up_c.wait_recv()

    @pl.when(has_next)
    def _():
        down_c.wait_recv()

    if static:
        zunits = [(s, h) for s in ORDER for h in range(HALVES)]
        units = [(0, h) for h in range(HALVES)] + zunits
        for i in range(len(units) + 1):
            if i < len(zunits):
                stage_z(*zunits[i])
            if i < len(units):
                stage_x(*units[i])
            if i < 2:
                wloads[i].wait()
                conv(ext[i], i)
            if i > 0:
                stage_c(*units[i - 1])
    else:
        pieces = range(HALVES)
        for t in range(2):
            wloads[t].wait()
            conv(ext[t], t)
        for h in pieces:
            stage_x(0, h)
        for h in pieces:
            stage_z(1, h)

        def body(step):
            for h in pieces:
                stage_z(step, h)
            for h in pieces:
                stage_x(step - 1, h)
            for h in pieces:
                stage_c(step - 2, h)

        loop(2, outer, body)
        for h in pieces:
            stage_x(outer - 1, h)
        for s in (outer - 2, outer - 1):
            for h in pieces:
                stage_c(s, h)

    loads[4].wait()
    loads[5].wait()
    loads[6].wait()
    mixed = (acc[...] / l_ref[...]).astype(BF16)
    attended = jnp.dot(mixed, wv[...], preferred_element_type=F32).astype(BF16)
    residual = src[...].astype(F32) + jnp.dot(attended, wo[...], preferred_element_type=F32)
    res_ref[...] = residual[width : width + tokens]
    v = _rms(residual, cg_ref[...].reshape(1, channels))
    activated = v / (1.0 + jnp.exp(-v))
    spot = lax.broadcasted_iota(jnp.int32, (total, 1), 0)
    start = jnp.where(has_prev, 0, width)
    stop = jnp.where(has_next, total, total - width)
    activated = jnp.where((spot >= start) & (spot < stop), activated, 0.0).astype(BF16)
    wloads[2].wait()
    conv(activated, 2)
    column = lax.broadcasted_iota(jnp.int32, (tokens, 1), 0) % width
    left = jnp.where(column == 0, 0.0, pltpu.roll(cacc[0], 1, 0))
    right = jnp.where(column == width - 1, 0.0, pltpu.roll(cacc[2], tokens - 1, 0))
    out_ref[...] = (left + cacc[1] + right).astype(BF16)

    for h in range(HALVES):
        if static:
            for s in (opening[1], 2):
                z_put(s, h).wait_send()
        loop(0, outer, lambda s: x_put(s, h).wait_send())
        loop(0, outer, lambda s: c_put(s, h, 0).wait_send())
        loop(0, outer, lambda s: c_put(s, h, 1).wait_send())

    @pl.when(has_next)
    def _():
        up_f.wait_send()
        up_c.wait_send()

    @pl.when(has_prev)
    def _():
        down_f.wait_send()
        down_c.wait_send()


def among(z, values):
    if all(v == values[0] for v in values):
        return values[0]
    out = values[-1]
    for i in range(len(values) - 1):
        out = jnp.where(z == i, values[i], out)
    return out


def column_plan():
    flips = {}
    for z in range(UNROLL):
        for q in range(UNROLL):
            relayed = any((q, z) in RELAY[a] for a in range(UNROLL))
            flips[z, q] = 0 if relayed else 1
    sends = {(a, b) for a in range(UNROLL) for b in DIRECT[a]}
    sends |= {(a, d) for a in range(UNROLL) for _, d in RELAY[a]}
    return flips, sends


def grid_kernel(
    count,
    width,
    feat_hbm,
    cache_hbm,
    ng_hbm,
    wq_hbm,
    wk_hbm,
    wv_hbm,
    wo_hbm,
    cg_hbm,
    cw_hbm,
    res_ref,
    out_ref,
    ng_ref,
    cg_ref,
    blocks,
    src,
    ext,
    wq,
    wk,
    wv,
    wo,
    wvo,
    cw,
    qs,
    m_ref,
    l_ref,
    acc,
    part_acc,
    part_ml,
    peer_acc,
    peer_ml,
    cacc,
    load_sem,
    cw_sem,
    halo_send,
    halo_recv,
    own_send,
    relay_send,
    x_send,
    recv,
    pair_send,
    pair_recv,
    reply,
):
    tokens, channels = feat_hbm.shape
    total = tokens + 2 * width
    half = tokens + width
    me = lax.axis_index("row")
    z = me // INNER
    x = (me // 2) % 2
    c = me % 2
    flips, sends = column_plan()
    planes = range(UNROLL)

    def at(zi, xi, ci):
        return zi * INNER + 2 * xi + ci

    xpeer = at(z, 1 - x, 1 - c)
    cpeer = at(z, x, 1 - c)
    has_prev = me > 0
    has_next = me < count - 1
    prev = jnp.maximum(me - 1, 0)
    after = jnp.minimum(me + 1, count - 1)
    down_plane = (x == 0) & (c == 0) & (z > 0)
    up_plane = (x == 1) & (c == 1) & (z < UNROLL - 1)

    def flagged(values):
        chosen = among(z, [int(v) for v in values])
        return bool(chosen) if isinstance(chosen, int) else chosen == 1

    def signal(sem, device):
        pl.semaphore_signal(sem, inc=1, device_id={"row": device}, device_id_type=MESH)

    def partners(a, b):
        return (a, b) in sends or (b, a) in sends

    barrier = pltpu.get_barrier_semaphore()
    for q in planes:
        @_when(flagged([q > a and partners(a, q) for a in planes]))
        def _():
            signal(barrier, at(q, x, 1 - c))

    @pl.when(x == 0)
    def _():
        signal(barrier, xpeer)

    @pl.when(c == 0)
    def _():
        signal(barrier, cpeer)

    @pl.when(up_plane)
    def _():
        signal(barrier, after)

    own = pl.ds(width, tokens)
    loads = [
        pltpu.make_async_copy(feat_hbm, src.at[own], load_sem.at[0]),
        pltpu.make_async_copy(wq_hbm, wq, load_sem.at[1]),
        pltpu.make_async_copy(wk_hbm, wk, load_sem.at[2]),
        pltpu.make_async_copy(cache_hbm, ext.at[:, own], load_sem.at[3]),
        pltpu.make_async_copy(wv_hbm, wv, load_sem.at[4]),
        pltpu.make_async_copy(wo_hbm, wo, load_sem.at[5]),
        pltpu.make_async_copy(cg_hbm, cg_ref, load_sem.at[6]),
        pltpu.make_async_copy(ng_hbm, ng_ref, load_sem.at[7]),
    ]
    wloads = [pltpu.make_async_copy(cw_hbm.at[t], cw.at[t], cw_sem.at[t]) for t in range(3)]
    loads[0].start()
    loads[7].start()

    lower = among(z, [sum(partners(q, a) for q in range(a)) for a in planes])

    @pl.when(me > 0)
    def _():
        pl.semaphore_wait(barrier, lower + x + c + jnp.where(down_plane, 1, 0))

    for q in planes[:-1]:
        @_when(flagged([q < a and (q, a) in sends for a in planes]))
        def _():
            signal(reply.at[z], at(q, x, 1 - c))

    @pl.when(x == 1)
    def _():
        signal(reply.at[UNROLL], xpeer)

    @pl.when(c == 1)
    def _():
        signal(reply.at[UNROLL + 1], cpeer)

    @pl.when(down_plane)
    def _():
        signal(reply.at[UNROLL + 2], prev)

    for copy in (loads[1], loads[2], loads[4], loads[5], loads[3], wloads[0], wloads[1], loads[6], wloads[2]):
        copy.start()

    def remote(a, b, send, receive, device):
        return pltpu.make_async_remote_copy(
            src_ref=a,
            dst_ref=b,
            send_sem=send,
            recv_sem=receive,
            device_id={"row": device},
            device_id_type=MESH,
        )

    def halo(a, b, index, device):
        return remote(a, b, halo_send.at[index], halo_recv.at[index], device)

    first = pl.ds(0, width)
    last = pl.ds(tokens - width, width)
    low = pl.ds(0, width)
    high = pl.ds(width + tokens, width)
    up_f = halo(feat_hbm.at[last], src.at[low], 0, after)
    down_f = halo(feat_hbm.at[first], src.at[high], 1, prev)
    up_c = halo(cache_hbm.at[:, last], ext.at[:, low], 2, after)
    down_c = halo(cache_hbm.at[:, first], ext.at[:, high], 3, prev)

    def put(ident, device, sem):
        part = blocks.at[ident]
        return remote(part, part, sem, recv.at[ident], device)

    def z_send(j):
        dest = among(z, [DIRECT[a][j] if j < len(DIRECT[a]) else 0 for a in planes])

        @_when(flagged([j < len(DIRECT[a]) for a in planes]))
        def _():
            @pl.when(dest > z)
            def _():
                pl.semaphore_wait(reply.at[dest], 1)

            put(me, at(dest, x, 1 - c), own_send.at[j]).start()

    def x_own():
        @pl.when(x == 0)
        def _():
            pl.semaphore_wait(reply.at[UNROLL], 1)

        put(me, xpeer, own_send.at[3]).start()

    def arrived(ident):
        put(ident, cpeer, own_send.at[0]).wait_recv()

    loads[0].wait()
    loads[7].wait()
    gain = ng_ref[...].reshape(1, channels)
    blocks[me] = _rms(src[own, :].astype(F32), gain).astype(BF16)
    z_send(0)
    z_send(1)
    x_own()

    @pl.when(c == 0)
    def _():
        pl.semaphore_wait(reply.at[UNROLL + 1], 1)

    @pl.when(up_plane)
    def _():
        pl.semaphore_wait(reply.at[UNROLL + 2], 1)

    @pl.when(has_next)
    def _():
        up_f.start()
        up_c.start()

    @pl.when(has_prev)
    def _():
        down_f.start()
        down_c.start()

    z_send(2)

    zero = jnp.zeros((width, channels), BF16)

    @pl.when(jnp.logical_not(has_prev))
    def _():
        src[low, :] = zero
        for t in range(ext.shape[0]):
            ext[t, low, :] = zero

    @pl.when(jnp.logical_not(has_next))
    def _():
        src[high, :] = zero
        for t in range(ext.shape[0]):
            ext[t, high, :] = zero

    def conv(frame, t):
        taps = jnp.concatenate(
            [frame[dy * width : dy * width + tokens] for dy in range(3)], axis=-1
        )
        for dx in range(3):
            part = jnp.dot(
                taps,
                cw[t, :, dx].reshape(3 * channels, channels),
                preferred_element_type=F32,
            )
            if t == 0:
                cacc[dx] = part
            else:
                cacc[dx] += part

    def attend(idents, opening=False):
        keys = jnp.concatenate([blocks[u] for u in idents], axis=0)
        scores = lax.dot_general(
            qs[...], keys, (((1,), (1,)), ((), ())), preferred_element_type=F32
        )
        peak = jnp.max(scores, axis=-1, keepdims=True)
        if opening:
            new = peak
        else:
            old = m_ref[...]
            new = jnp.maximum(old, peak)
            scale = jnp.exp2(old - new)
        expw = jnp.exp2(scores - new)
        m_ref[...] = new
        mass = jnp.sum(expw, axis=-1, keepdims=True)
        value = jnp.dot(expw.astype(BF16), keys, preferred_element_type=F32)
        if opening:
            l_ref[...] = mass
            acc[...] = value
        else:
            l_ref[...] = l_ref[...] * scale + mass
            acc[...] = acc[...] * scale + value

    def column(j):
        q = among(z, [ARRIVE[a][j] for a in planes])
        flip = among(z, [flips[a, ARRIVE[a][j]] for a in planes])
        return q, c + flip - 2 * c * flip

    def stage_z(j):
        q, core = column(j)
        ident = at(q, x, core)
        arrived(ident)
        if any(RELAY.values()):
            relayed = among(z, [RELAY[a][0][0] if RELAY[a] else UNROLL for a in planes])
            dest = among(z, [RELAY[a][0][1] if RELAY[a] else 0 for a in planes])

            @pl.when(q == relayed)
            def _():
                put(ident, at(dest, x, 1 - c), relay_send.at[0]).start()

        put(ident, xpeer, x_send.at[j]).start()
        return ident

    def stage_x(j):
        q, core = column(j)
        ident = at(q, 1 - x, 1 - core)
        arrived(ident)
        return ident


    loads[4].wait()
    loads[5].wait()
    wvo[...] = jnp.dot(wv[...], wo[...], preferred_element_type=F32).astype(BF16)
    z0 = stage_z(0)
    z1 = stage_z(1)
    @pl.when(has_prev)
    def _():
        up_f.wait_recv()

    @pl.when(has_next)
    def _():
        down_f.wait_recv()

    loads[1].wait()
    loads[2].wait()
    mine = pl.ds(pl.multiple_of(c * half, 16), half)
    rows = src[pl.ds(pl.multiple_of(c * width, 16), half), :].astype(F32)
    query = jnp.dot(_rms(rows, gain).astype(BF16), wq[...], preferred_element_type=F32).astype(BF16)
    folded = lax.dot_general(
        query, wk[...], (((1,), (1,)), ((), ())), preferred_element_type=F32
    )
    qs[mine, :] = (folded * (channels**-0.5 * math.log2(math.e))).astype(BF16)
    share = remote(qs.at[mine], qs.at[mine], pair_send.at[0], pair_recv.at[0], cpeer)
    share.start()
    z2 = stage_z(2)
    loads[3].wait()

    @pl.when(has_prev)
    def _():
        up_c.wait_recv()

    @pl.when(has_next)
    def _():
        down_c.wait_recv()

    for t in range(2):
        wloads[t].wait()
        conv(ext[t], t)
    arrived(xpeer)
    share.wait_recv()
    attend([me, xpeer], True)
    attend([z0, z1])
    x0 = stage_x(0)
    attend([z2, x0])
    x1 = stage_x(1)
    x2 = stage_x(2)
    attend([x1, x2])

    theirs = pl.ds(pl.multiple_of((1 - c) * tokens, 16), total)
    window = pl.ds(pl.multiple_of(c * tokens, 16), total)
    part_acc[...] = acc[theirs, :].astype(BF16)
    lane = lax.broadcasted_iota(jnp.int32, part_ml.shape, 1)
    part_ml[...] = jnp.where(lane < part_ml.shape[1] // 2, m_ref[theirs, :], l_ref[theirs, :])
    give = [
        remote(part_acc, peer_acc, pair_send.at[1], pair_recv.at[1], cpeer),
        remote(part_ml, peer_ml, pair_send.at[2], pair_recv.at[2], cpeer),
    ]
    for copy in give:
        copy.start()

    for j in range(3):
        @_when(flagged([j < len(DIRECT[a]) for a in planes]))
        def _():
            put(me, cpeer, own_send.at[j]).wait_send()

        put(me, cpeer, x_send.at[j]).wait_send()
    put(me, cpeer, own_send.at[3]).wait_send()

    @_when(flagged([bool(RELAY[a]) for a in planes]))
    def _():
        put(me, cpeer, relay_send.at[0]).wait_send()

    @pl.when(has_next)
    def _():
        up_f.wait_send()
        up_c.wait_send()

    @pl.when(has_prev)
    def _():
        down_f.wait_send()
        down_c.wait_send()

    share.wait_send()
    loads[6].wait()
    wloads[2].wait()
    for copy in give:
        copy.wait()

    peer_m = peer_ml[:, :1]
    peer_l = peer_ml[:, part_ml.shape[1] // 2 :][:, :1]
    own_m = m_ref[window, :]
    new = jnp.maximum(own_m, peer_m)
    own_w = jnp.exp2(own_m - new)
    peer_w = jnp.exp2(peer_m - new)
    inverse = 1.0 / (l_ref[window, :] * own_w + peer_l * peer_w)
    mixed = acc[window, :] * (own_w * inverse) + peer_acc[...].astype(F32) * (peer_w * inverse)
    residual = src[...].astype(F32) + jnp.dot(
        mixed.astype(BF16), wvo[...], preferred_element_type=F32
    )
    res_ref[...] = residual[width : width + tokens]
    v = _rms(residual, cg_ref[...].reshape(1, channels))
    activated = v / (1.0 + jnp.exp(-v))
    spot = lax.broadcasted_iota(jnp.int32, (total, 1), 0)
    start = jnp.where(has_prev, 0, width)
    stop = jnp.where(has_next, total, total - width)
    activated = jnp.where((spot >= start) & (spot < stop), activated, 0.0).astype(BF16)
    conv(activated, 2)
    column_of = lax.broadcasted_iota(jnp.int32, (tokens, 1), 0) % width
    left = jnp.where(column_of == 0, 0.0, pltpu.roll(cacc[0], 1, 0))
    right = jnp.where(column_of == width - 1, 0.0, pltpu.roll(cacc[2], tokens - 1, 0))
    out_ref[...] = (left + cacc[1] + right).astype(BF16)


def settle(residual, conv_out, residual_hbm, out_hbm, sem):
    copies = [
        pltpu.make_async_copy(residual, residual_hbm, sem.at[0]),
        pltpu.make_async_copy(conv_out, out_hbm, sem.at[1]),
    ]
    for copy in copies:
        copy.start()
    for copy in copies:
        copy.wait()


def shards(features, conv_cache, norm_gain, w_query, w_key, w_value, w_out, conv_gain, conv_weight):
    frames, rows, width, channels = features.shape
    cached = conv_cache.shape[0]
    tokens = rows * width
    total = tokens + 2 * width
    count = lax.axis_size("row")
    outer = count // INNER
    hbm = pl.BlockSpec(memory_space=pltpu.HBM)
    vmem = pl.BlockSpec(memory_space=pltpu.VMEM)
    dma = pltpu.SemaphoreType.DMA
    square = pltpu.VMEM((channels, channels), BF16)
    lead = [pltpu.VMEM((channels,), F32), pltpu.VMEM((channels,), F32), pltpu.VMEM((count, tokens, channels), BF16)]
    lead += [pltpu.VMEM((total, channels), BF16), pltpu.VMEM((cached, total, channels), BF16)]
    lead += [square, square, square, square]
    kernels = pltpu.VMEM(conv_weight.shape, BF16)
    summed = pltpu.VMEM((3, tokens, channels), F32)
    if outer == UNROLL:
        body = grid_kernel
        both = 2 * (tokens + width)
        lanes = 128
        scratch = lead + [
            square,
            kernels,
            pltpu.VMEM((both, channels), BF16),
            pltpu.VMEM((both, 1), F32),
            pltpu.VMEM((both, 1), F32),
            pltpu.VMEM((both, channels), F32),
            pltpu.VMEM((total, channels), BF16),
            pltpu.VMEM((total, lanes), F32),
            pltpu.VMEM((total, channels), BF16),
            pltpu.VMEM((total, lanes), F32),
            summed,
            dma((8,)),
            dma((3,)),
            dma((4,)),
            dma((4,)),
            dma((4,)),
            dma((1,)),
            dma((3,)),
            dma((count,)),
            dma((3,)),
            dma((3,)),
            pltpu.SemaphoreType.REGULAR((UNROLL + 3,)),
        ]
    else:
        body = ring
        scratch = lead + [
            kernels,
            pltpu.VMEM((total, channels), BF16),
            pltpu.VMEM((total, 1), F32),
            pltpu.VMEM((total, 1), F32),
            pltpu.VMEM((total, channels), F32),
            summed,
            dma((8,)),
            dma((3,)),
            dma((4,)),
            dma((4,)),
            dma((outer, HALVES)),
            dma((outer, HALVES)),
            dma((2, outer, HALVES)),
            dma((count, HALVES)),
        ]
    residual, conv_out = pl.pallas_call(
        functools.partial(body, count, width),
        out_shape=(
            jax.ShapeDtypeStruct((tokens, channels), F32),
            jax.ShapeDtypeStruct((tokens, channels), BF16),
        ),
        in_specs=[hbm] * 9,
        out_specs=(vmem, vmem),
        scratch_shapes=scratch,
        compiler_params=pltpu.CompilerParams(
            collective_id=0, has_side_effects=True, vmem_limit_bytes=48 << 20
        ),
    )(
        *(
            pltpu.with_memory_space_constraint(x, pltpu.HBM)
            for x in (
                features.reshape(tokens, channels),
                conv_cache.reshape(cached, tokens, channels),
                norm_gain,
                w_query,
                w_key,
                w_value,
                w_out,
                conv_gain,
                conv_weight,
            )
        )
    )
    residual, conv_out = pl.pallas_call(
        settle,
        out_shape=(
            jax.ShapeDtypeStruct((tokens, channels), F32),
            jax.ShapeDtypeStruct((tokens, channels), BF16),
        ),
        in_specs=[vmem, vmem],
        out_specs=(hbm, hbm),
        scratch_shapes=[dma((2,))],
    )(*(pltpu.with_memory_space_constraint(a, pltpu.VMEM) for a in (residual, conv_out)))
    return (
        residual.reshape(frames, rows, width, channels),
        conv_out.reshape(frames, rows, width, channels),
    )


def solution(mesh):
    placed = (
        P(None, ("clip", "row"), None, None),
        P(None, ("clip", "row"), None, None),
        P(),
        P(),
        P(),
        P(),
        P(),
        P(),
        P(),
    )
    return jax.shard_map(
        shards,
        mesh=mesh,
        in_specs=placed,
        out_specs=(P(None, ("clip", "row"), None, None), P(None, ("clip", "row"), None, None)),
        check_vma=False,
    )
```

```python
import functools
import math

import jax
import jax.numpy as jnp
from jax import lax
from jax.experimental import pallas as pl
from jax.experimental.pallas import tpu as pltpu
from jax.sharding import PartitionSpec as P

MESH = pl.DeviceIdType.MESH
F32 = jnp.float32
BF16 = jnp.bfloat16
INNER = 4
UNROLL = 4
HALVES = 1
ORDER = (3, 1, 2)
DIRECT = {0: (1, 2, 3), 1: (0, 2), 2: (1, 0, 3), 3: (0, 2)}
RELAY = {0: ((3, 1),), 1: (), 2: ((1, 3),), 3: ()}
SIDE = {0: 1, 1: 2, 2: 1, 3: 2}
ARRIVE = {0: (1, 3, 2), 1: (0, 2, 3), 2: (1, 0, 3), 3: (2, 0, 1)}


def _rms(v, gain):
    return v * lax.rsqrt(jnp.mean(v * v, axis=-1, keepdims=True) + 1e-06) * gain


def _flip(index, bits):
    bit = 1
    while bit <= bits:
        if bits & bit:
            index = index + bit - 2 * bit * ((index // bit) % 2)
        bit *= 2
    return index


def _when(cond):
    if isinstance(cond, bool):
        return (lambda f: f()) if cond else (lambda f: None)
    return pl.when(cond)


def _both(a, b):
    if isinstance(a, bool) and isinstance(b, bool):
        return a and b
    return jnp.logical_and(a, b)


def ring(
    count,
    width,
    feat_hbm,
    cache_hbm,
    ng_hbm,
    wq_hbm,
    wk_hbm,
    wv_hbm,
    wo_hbm,
    cg_hbm,
    cw_hbm,
    res_ref,
    out_ref,
    ng_ref,
    cg_ref,
    blocks,
    src,
    ext,
    wq,
    wk,
    wv,
    wo,
    cw,
    qs,
    m_ref,
    l_ref,
    acc,
    cacc,
    load_sem,
    cw_sem,
    halo_send,
    halo_recv,
    z_send,
    x_send,
    c_send,
    recv,
):
    outer = count // INNER
    tokens, channels = feat_hbm.shape
    total = tokens + 2 * width
    me = lax.axis_index("row")
    z = me // INNER
    xpeer = me - z * INNER
    pair = (xpeer // 2) % 2
    core = xpeer % 2
    xpeer = me + 2 - 4 * pair
    cpeer = me + 1 - 2 * core
    static = outer == UNROLL
    piece = tokens // HALVES

    def zpeer(step):
        if static:
            return _flip(z, step)
        return lax.rem(z + step, outer)

    def zfrom(step):
        if static:
            return _flip(z, step)
        return lax.rem(z - step + outer, outer)

    def loop(low, high, body):
        if static:
            for step in range(low, high):
                body(step)
        else:
            lax.fori_loop(low, high, lambda i, carry: (body(i), carry)[1], 0)

    has_prev = me > 0
    has_next = me < count - 1
    prev = jnp.maximum(me - 1, 0)
    after = jnp.minimum(me + 1, count - 1)

    own = pl.ds(width, tokens)
    loads = [
        pltpu.make_async_copy(feat_hbm, src.at[own], load_sem.at[0]),
        pltpu.make_async_copy(wq_hbm, wq, load_sem.at[1]),
        pltpu.make_async_copy(wk_hbm, wk, load_sem.at[2]),
        pltpu.make_async_copy(cache_hbm, ext.at[:, own], load_sem.at[3]),
        pltpu.make_async_copy(wv_hbm, wv, load_sem.at[4]),
        pltpu.make_async_copy(wo_hbm, wo, load_sem.at[5]),
        pltpu.make_async_copy(cg_hbm, cg_ref, load_sem.at[6]),
    ]
    gains = pltpu.make_async_copy(ng_hbm, ng_ref, load_sem.at[7])
    gains.start()
    wloads = [pltpu.make_async_copy(cw_hbm.at[t], cw.at[t], cw_sem.at[t]) for t in range(3)]
    for copy in loads[:4]:
        copy.start()
    for copy in wloads[:2]:
        copy.start()
    for copy in loads[4:]:
        copy.start()
    wloads[2].start()

    barrier = pltpu.get_barrier_semaphore()

    def greet(device):
        pl.semaphore_signal(barrier, inc=1, device_id={"row": device}, device_id_type=MESH)

    def greet_z(step):
        greet(zpeer(step) * INNER + 2 * pair + core)

    loop(1, outer, greet_z)
    greet(xpeer)
    greet(cpeer)

    greet(lax.rem(me + 1, count))
    greet(lax.rem(me + count - 1, count))
    pl.semaphore_wait(barrier, outer + 3)

    def halo(a, b, index, device):
        return pltpu.make_async_remote_copy(
            src_ref=a,
            dst_ref=b,
            send_sem=halo_send.at[index],
            recv_sem=halo_recv.at[index],
            device_id={"row": device},
            device_id_type=MESH,
        )

    first = pl.ds(0, width)
    last = pl.ds(tokens - width, width)
    low = pl.ds(0, width)
    high = pl.ds(width + tokens, width)
    up_f = halo(feat_hbm.at[last], src.at[low], 0, after)
    down_f = halo(feat_hbm.at[first], src.at[high], 1, prev)
    up_c = halo(cache_hbm.at[:, last], ext.at[:, low], 2, after)
    down_c = halo(cache_hbm.at[:, first], ext.at[:, high], 3, prev)

    @pl.when(has_next)
    def _():
        up_f.start()

    @pl.when(has_prev)
    def _():
        down_f.start()

    def put(ident, h, sem, device):
        part = blocks.at[ident, pl.ds(h * piece, piece)]
        return pltpu.make_async_remote_copy(
            src_ref=part,
            dst_ref=part,
            send_sem=sem,
            recv_sem=recv.at[ident, h],
            device_id={"row": device},
            device_id_type=MESH,
        )

    def at(zi, p, c):
        return zi * INNER + 2 * p + c

    def z_put(step, h):
        if static and step == 2:
            return put(at(zpeer(3), pair, core), h, z_send.at[2, h], at(zpeer(1), pair, core))
        return put(me, h, z_send.at[step, h], at(zpeer(step), pair, core))

    def x_put(step, h):
        return put(at(zfrom(step), pair, core), h, x_send.at[step, h], xpeer)

    def c_put(step, h, which):
        p = pair if which == 0 else 1 - pair
        return put(at(zfrom(step), p, core), h, c_send.at[which, step, h], cpeer)

    def arrived(ident, h):
        put(ident, h, z_send.at[0, h], cpeer).wait_recv()

    gains.wait()
    gain = ng_ref[...].reshape(1, channels)
    loads[0].wait()
    blocks[me] = _rms(src[own, :].astype(F32), gain).astype(BF16)
    opening = [s for s in ORDER if s != 2] if static else range(1, min(outer, 3))
    for s in opening:
        for h in range(HALVES):
            if s == opening[0] or not static:
                z_put(s, h).start()
            if s == opening[0]:
                x_put(0, h).start()
    for h in range(HALVES):
        c_put(0, h, 0).start()

    @pl.when(has_next)
    def _():
        up_c.start()

    @pl.when(has_prev)
    def _():
        down_c.start()

    zero = jnp.zeros((width, channels), BF16)

    @pl.when(has_prev)
    def _():
        up_f.wait_recv()

    @pl.when(jnp.logical_not(has_prev))
    def _():
        src[low, :] = zero
        for t in range(ext.shape[0]):
            ext[t, low, :] = zero

    @pl.when(has_next)
    def _():
        down_f.wait_recv()

    @pl.when(jnp.logical_not(has_next))
    def _():
        src[high, :] = zero
        for t in range(ext.shape[0]):
            ext[t, high, :] = zero

    if static:
        z_put(opening[0], 0).wait_send()
        z_put(opening[1], 0).start()
    loads[1].wait()
    loads[2].wait()
    normed = _rms(src[...].astype(F32), gain).astype(BF16)
    query = jnp.dot(normed, wq[...], preferred_element_type=F32).astype(BF16)
    folded = lax.dot_general(
        query, wk[...], (((1,), (1,)), ((), ())), preferred_element_type=F32
    )
    qs[...] = (folded * (channels**-0.5 * math.log2(math.e))).astype(BF16)
    m_ref[...] = jnp.full(m_ref.shape, -1e30, F32)
    l_ref[...] = jnp.zeros(l_ref.shape, F32)
    acc[...] = jnp.zeros(acc.shape, F32)

    def conv(frame, t):
        taps = jnp.concatenate(
            [frame[dy * width : dy * width + tokens] for dy in range(3)], axis=-1
        )
        for dx in range(3):
            part = jnp.dot(
                taps,
                cw[t, :, dx].reshape(3 * channels, channels),
                preferred_element_type=F32,
            )
            if t == 0:
                cacc[dx] = part
            else:
                cacc[dx] += part

    def attend(step):
        zi = zfrom(step)
        keys = blocks[pl.ds(zi * INNER, INNER)].reshape(INNER * tokens, channels)
        scores = lax.dot_general(
            qs[...], keys, (((1,), (1,)), ((), ())), preferred_element_type=F32
        )
        old = m_ref[...]
        new = jnp.maximum(old, jnp.max(scores, axis=-1, keepdims=True))
        scale = jnp.exp2(old - new)
        expw = jnp.exp2(scores - new)
        m_ref[...] = new
        l_ref[...] = l_ref[...] * scale + jnp.sum(expw, axis=-1, keepdims=True)
        acc[...] = acc[...] * scale + jnp.dot(
            expw.astype(BF16), keys, preferred_element_type=F32
        )

    def stage_z(step, h):
        if not static:
            z_put(step, h).wait_send()

            @pl.when(step + 2 < outer)
            def _():
                z_put(step + 2, h).start()

        arrived(at(zfrom(step), pair, core), h)
        if static and step == 3:
            z_put(2, h).start()
        x_put(step, h).start()
        c_put(step, h, 0).start()

    def stage_x(step, h):
        arrived(at(zfrom(step), 1 - pair, core), h)
        c_put(step, h, 1).start()

    def stage_c(step, h):
        zi = zfrom(step)
        arrived(at(zi, pair, 1 - core), h)
        arrived(at(zi, 1 - pair, 1 - core), h)
        if h == HALVES - 1:
            attend(step)

    loads[3].wait()

    @pl.when(has_prev)
    def _():
        up_c.wait_recv()

    @pl.when(has_next)
    def _():
        down_c.wait_recv()

    if static:
        zunits = [(s, h) for s in ORDER for h in range(HALVES)]
        units = [(0, h) for h in range(HALVES)] + zunits
        for i in range(len(units) + 1):
            if i < len(zunits):
                stage_z(*zunits[i])
            if i < len(units):
                stage_x(*units[i])
            if i < 2:
                wloads[i].wait()
                conv(ext[i], i)
            if i > 0:
                stage_c(*units[i - 1])
    else:
        pieces = range(HALVES)
        for t in range(2):
            wloads[t].wait()
            conv(ext[t], t)
        for h in pieces:
            stage_x(0, h)
        for h in pieces:
            stage_z(1, h)

        def body(step):
            for h in pieces:
                stage_z(step, h)
            for h in pieces:
                stage_x(step - 1, h)
            for h in pieces:
                stage_c(step - 2, h)

        loop(2, outer, body)
        for h in pieces:
            stage_x(outer - 1, h)
        for s in (outer - 2, outer - 1):
            for h in pieces:
                stage_c(s, h)

    loads[4].wait()
    loads[5].wait()
    loads[6].wait()
    mixed = (acc[...] / l_ref[...]).astype(BF16)
    attended = jnp.dot(mixed, wv[...], preferred_element_type=F32).astype(BF16)
    residual = src[...].astype(F32) + jnp.dot(attended, wo[...], preferred_element_type=F32)
    res_ref[...] = residual[width : width + tokens]
    v = _rms(residual, cg_ref[...].reshape(1, channels))
    activated = v / (1.0 + jnp.exp(-v))
    spot = lax.broadcasted_iota(jnp.int32, (total, 1), 0)
    start = jnp.where(has_prev, 0, width)
    stop = jnp.where(has_next, total, total - width)
    activated = jnp.where((spot >= start) & (spot < stop), activated, 0.0).astype(BF16)
    wloads[2].wait()
    conv(activated, 2)
    column = lax.broadcasted_iota(jnp.int32, (tokens, 1), 0) % width
    left = jnp.where(column == 0, 0.0, pltpu.roll(cacc[0], 1, 0))
    right = jnp.where(column == width - 1, 0.0, pltpu.roll(cacc[2], tokens - 1, 0))
    out_ref[...] = (left + cacc[1] + right).astype(BF16)

    for h in range(HALVES):
        if static:
            for s in (opening[1], 2):
                z_put(s, h).wait_send()
        loop(0, outer, lambda s: x_put(s, h).wait_send())
        loop(0, outer, lambda s: c_put(s, h, 0).wait_send())
        loop(0, outer, lambda s: c_put(s, h, 1).wait_send())

    @pl.when(has_next)
    def _():
        up_f.wait_send()
        up_c.wait_send()

    @pl.when(has_prev)
    def _():
        down_f.wait_send()
        down_c.wait_send()


def among(z, values):
    if all(v == values[0] for v in values):
        return values[0]
    out = values[-1]
    for i in range(len(values) - 1):
        out = jnp.where(z == i, values[i], out)
    return out


def column_plan():
    flips = {}
    for z in range(UNROLL):
        for q in range(UNROLL):
            relayed = any((q, z) in RELAY[a] for a in range(UNROLL))
            flips[z, q] = 0 if relayed else 1
    sends = {(a, b) for a in range(UNROLL) for b in DIRECT[a]}
    sends |= {(a, d) for a in range(UNROLL) for _, d in RELAY[a]}
    return flips, sends


def grid_kernel(
    count,
    width,
    feat_hbm,
    cache_hbm,
    ng_hbm,
    wq_hbm,
    wk_hbm,
    wv_hbm,
    wo_hbm,
    cg_hbm,
    cw_hbm,
    res_ref,
    out_ref,
    ng_ref,
    cg_ref,
    blocks,
    src,
    ext,
    wq,
    wk,
    wv,
    wo,
    wvo,
    cw,
    qs,
    m_ref,
    l_ref,
    acc,
    part_acc,
    part_ml,
    peer_acc,
    peer_ml,
    cacc,
    load_sem,
    cw_sem,
    halo_send,
    halo_recv,
    own_send,
    relay_send,
    x_send,
    side_send,
    late_send,
    recv,
    pair_send,
    pair_recv,
    reply,
):
    tokens, channels = feat_hbm.shape
    total = tokens + 2 * width
    half = tokens + width
    me = lax.axis_index("row")
    z = me // INNER
    x = (me // 2) % 2
    c = me % 2
    flips, sends = column_plan()
    planes = range(UNROLL)

    def at(zi, xi, ci):
        return zi * INNER + 2 * xi + ci

    xpeer = at(z, 1 - x, 1 - c)
    cpeer = at(z, x, 1 - c)
    has_prev = me > 0
    has_next = me < count - 1
    prev = jnp.maximum(me - 1, 0)
    after = jnp.minimum(me + 1, count - 1)
    down_plane = (x == 0) & (c == 0) & (z > 0)
    up_plane = (x == 1) & (c == 1) & (z < UNROLL - 1)

    def flagged(values):
        chosen = among(z, [int(v) for v in values])
        return bool(chosen) if isinstance(chosen, int) else chosen == 1

    def signal(sem, device):
        pl.semaphore_signal(sem, inc=1, device_id={"row": device}, device_id_type=MESH)

    def partners(a, b):
        return (a, b) in sends or (b, a) in sends

    barrier = pltpu.get_barrier_semaphore()
    for q in planes:
        @_when(flagged([q > a and partners(a, q) for a in planes]))
        def _():
            signal(barrier, at(q, x, 1 - c))

    @pl.when(x == 0)
    def _():
        signal(barrier, xpeer)

    @pl.when(c == 0)
    def _():
        signal(barrier, cpeer)

    @pl.when(up_plane)
    def _():
        signal(barrier, after)

    own = pl.ds(width, tokens)
    loads = [
        pltpu.make_async_copy(feat_hbm, src.at[own], load_sem.at[0]),
        pltpu.make_async_copy(wq_hbm, wq, load_sem.at[1]),
        pltpu.make_async_copy(wk_hbm, wk, load_sem.at[2]),
        pltpu.make_async_copy(cache_hbm, ext.at[:, own], load_sem.at[3]),
        pltpu.make_async_copy(wv_hbm, wv, load_sem.at[4]),
        pltpu.make_async_copy(wo_hbm, wo, load_sem.at[5]),
        pltpu.make_async_copy(cg_hbm, cg_ref, load_sem.at[6]),
        pltpu.make_async_copy(ng_hbm, ng_ref, load_sem.at[7]),
    ]
    wloads = [pltpu.make_async_copy(cw_hbm.at[t], cw.at[t], cw_sem.at[t]) for t in range(3)]
    loads[0].start()
    loads[7].start()

    lower = among(z, [sum(partners(q, a) for q in range(a)) for a in planes])

    @pl.when(me > 0)
    def _():
        pl.semaphore_wait(barrier, lower + x + c + jnp.where(down_plane, 1, 0))

    for q in planes[:-1]:
        @_when(flagged([q < a and (q, a) in sends for a in planes]))
        def _():
            signal(reply.at[z], at(q, x, 1 - c))

    @pl.when(x == 1)
    def _():
        signal(reply.at[UNROLL], xpeer)

    @pl.when(c == 1)
    def _():
        signal(reply.at[UNROLL + 1], cpeer)

    @pl.when(down_plane)
    def _():
        signal(reply.at[UNROLL + 2], prev)

    for copy in (loads[1], loads[2], loads[4], loads[5], loads[3], wloads[0], wloads[1], loads[6], wloads[2]):
        copy.start()

    def remote(a, b, send, receive, device):
        return pltpu.make_async_remote_copy(
            src_ref=a,
            dst_ref=b,
            send_sem=send,
            recv_sem=receive,
            device_id={"row": device},
            device_id_type=MESH,
        )

    def halo(a, b, index, device):
        return remote(a, b, halo_send.at[index], halo_recv.at[index], device)

    first = pl.ds(0, width)
    last = pl.ds(tokens - width, width)
    low = pl.ds(0, width)
    high = pl.ds(width + tokens, width)
    up_f = halo(feat_hbm.at[last], src.at[low], 0, after)
    down_f = halo(feat_hbm.at[first], src.at[high], 1, prev)
    up_c = halo(cache_hbm.at[:, last], ext.at[:, low], 2, after)
    down_c = halo(cache_hbm.at[:, first], ext.at[:, high], 3, prev)

    def put(ident, device, sem):
        part = blocks.at[ident]
        return remote(part, part, sem, recv.at[ident], device)

    def z_send(j):
        dest = among(z, [DIRECT[a][j] if j < len(DIRECT[a]) else 0 for a in planes])

        @_when(flagged([j < len(DIRECT[a]) for a in planes]))
        def _():
            @pl.when(dest > z)
            def _():
                pl.semaphore_wait(reply.at[dest], 1)

            put(me, at(dest, x, 1 - c), own_send.at[j]).start()

    def x_own():
        @pl.when(x == 0)
        def _():
            pl.semaphore_wait(reply.at[UNROLL], 1)

        put(me, xpeer, own_send.at[3]).start()

    def arrived(ident):
        put(ident, cpeer, own_send.at[0]).wait_recv()

    loads[0].wait()
    loads[7].wait()
    gain = ng_ref[...].reshape(1, channels)
    blocks[me] = _rms(src[own, :].astype(F32), gain).astype(BF16)
    z_send(0)
    z_send(1)
    x_own()

    @pl.when(c == 0)
    def _():
        pl.semaphore_wait(reply.at[UNROLL + 1], 1)

    @pl.when(up_plane)
    def _():
        pl.semaphore_wait(reply.at[UNROLL + 2], 1)

    @pl.when(has_next)
    def _():
        up_f.start()

    @pl.when(has_prev)
    def _():
        down_f.start()

    @pl.when(has_next)
    def _():
        up_c.start()

    @pl.when(has_prev)
    def _():
        down_c.start()

    z_send(2)

    zero = jnp.zeros((width, channels), BF16)

    @pl.when(jnp.logical_not(has_prev))
    def _():
        src[low, :] = zero
        for t in range(ext.shape[0]):
            ext[t, low, :] = zero

    @pl.when(jnp.logical_not(has_next))
    def _():
        src[high, :] = zero
        for t in range(ext.shape[0]):
            ext[t, high, :] = zero

    def conv(frame, t):
        taps = jnp.concatenate(
            [frame[dy * width : dy * width + tokens] for dy in range(3)], axis=-1
        )
        for dx in range(3):
            part = jnp.dot(
                taps,
                cw[t, :, dx].reshape(3 * channels, channels),
                preferred_element_type=F32,
            )
            if t == 0:
                cacc[dx] = part
            else:
                cacc[dx] += part

    def attend(idents, rows=slice(None), opening=False):
        keys = jnp.concatenate([blocks[u] for u in idents], axis=0)
        scores = lax.dot_general(
            qs[rows, :], keys, (((1,), (1,)), ((), ())), preferred_element_type=F32
        )
        peak = jnp.max(scores, axis=-1, keepdims=True)
        if opening:
            new = peak
        else:
            old = m_ref[rows, :]
            new = jnp.maximum(old, peak)
            scale = jnp.exp2(old - new)
        expw = jnp.exp2(scores - new)
        m_ref[rows, :] = new
        mass = jnp.sum(expw, axis=-1, keepdims=True)
        value = jnp.dot(expw.astype(BF16), keys, preferred_element_type=F32)
        if opening:
            l_ref[rows, :] = mass
            acc[rows, :] = value
        else:
            l_ref[rows, :] = l_ref[rows, :] * scale + mass
            acc[rows, :] = acc[rows, :] * scale + value

    def column(j):
        q = among(z, [ARRIVE[a][j] for a in planes])
        flip = among(z, [flips[a, ARRIVE[a][j]] for a in planes])
        return q, c + flip - 2 * c * flip

    def stage_z(j):
        q, core = column(j)
        ident = at(q, x, core)
        arrived(ident)
        if any(RELAY.values()):
            relayed = among(z, [RELAY[a][0][0] if RELAY[a] else UNROLL for a in planes])
            dest = among(z, [RELAY[a][0][1] if RELAY[a] else 0 for a in planes])

            @pl.when(q == relayed)
            def _():
                put(ident, at(dest, x, 1 - c), relay_send.at[0]).start()

        @_when(flagged([ARRIVE[a][j] != SIDE[a] for a in planes]))
        def _():
            put(ident, xpeer, x_send.at[j]).start()

        return ident

    def stage_side():
        arrived(xpeer)
        for step in (-1, 1):
            @_when(flagged([SIDE.get(a + step) == a for a in planes]))
            def _():
                put(xpeer, at(z + step, x, 1 - c), side_send.at[(step + 1) // 2]).start()

    def stage_x(j):
        q, core = column(j)
        ident = at(q, 1 - x, 1 - core)
        arrived(ident)
        return ident

    def stage_late(j):
        ident = stage_x(j)
        put(ident, cpeer, late_send.at[j]).start()
        return ident

    def stage_peer(j):
        q, core = column(j)
        ident = at(q, 1 - x, core)
        arrived(ident)
        return ident

    loads[4].wait()
    loads[5].wait()
    wvo[...] = jnp.dot(wv[...], wo[...], preferred_element_type=F32).astype(BF16)
    z0 = stage_z(0)
    stage_side()
    z1 = stage_z(1)
    @pl.when(has_prev)
    def _():
        up_f.wait_recv()

    @pl.when(has_next)
    def _():
        down_f.wait_recv()

    loads[1].wait()
    loads[2].wait()
    mine = pl.ds(pl.multiple_of(c * half, 16), half)
    rows = src[pl.ds(pl.multiple_of(c * width, 16), half), :].astype(F32)
    query = jnp.dot(_rms(rows, gain).astype(BF16), wq[...], preferred_element_type=F32).astype(BF16)
    folded = lax.dot_general(
        query, wk[...], (((1,), (1,)), ((), ())), preferred_element_type=F32
    )
    qs[mine, :] = (folded * (channels**-0.5 * math.log2(math.e))).astype(BF16)
    share = remote(qs.at[mine], qs.at[mine], pair_send.at[0], pair_recv.at[0], cpeer)
    share.start()
    z2 = stage_z(2)
    share.wait_recv()
    attend([me, xpeer, z0, z1], opening=True)
    loads[3].wait()

    @pl.when(has_prev)
    def _():
        up_c.wait_recv()

    @pl.when(has_next)
    def _():
        down_c.wait_recv()

    wloads[0].wait()
    conv(ext[0], 0)
    x0 = stage_x(0)
    attend([z2, x0])
    theirs = pl.ds(pl.multiple_of((1 - c) * tokens, 16), total)
    window = pl.ds(pl.multiple_of(c * tokens, 16), total)
    part_acc[...] = acc[theirs, :].astype(BF16)
    lane = lax.broadcasted_iota(jnp.int32, part_ml.shape, 1)
    part_ml[...] = jnp.where(lane < part_ml.shape[1] // 2, m_ref[theirs, :], l_ref[theirs, :])
    give = [
        remote(part_acc, peer_acc, pair_send.at[1], pair_recv.at[1], cpeer),
        remote(part_ml, peer_ml, pair_send.at[2], pair_recv.at[2], cpeer),
    ]
    for copy in give:
        copy.start()

    def merge():
        for copy in give:
            copy.wait_recv()
        peer_m = peer_ml[:, :1]
        peer_l = peer_ml[:, part_ml.shape[1] // 2 :][:, :1]
        own_m = m_ref[window, :]
        new = jnp.maximum(own_m, peer_m)
        own_w = jnp.exp2(own_m - new)
        peer_w = jnp.exp2(peer_m - new)
        m_ref[window, :] = new
        l_ref[window, :] = l_ref[window, :] * own_w + peer_l * peer_w
        acc[window, :] = acc[window, :] * own_w + peer_acc[...].astype(F32) * peer_w

    wloads[1].wait()
    conv(ext[1], 1)
    x1 = stage_late(1)
    x2 = stage_late(2)
    merge()
    attend([x1, x2], window)
    for j in range(3):
        @_when(flagged([j < len(DIRECT[a]) for a in planes]))
        def _():
            put(me, cpeer, own_send.at[j]).wait_send()

        @_when(flagged([ARRIVE[a][j] != SIDE[a] for a in planes]))
        def _():
            put(me, cpeer, x_send.at[j]).wait_send()

    for step in (-1, 1):
        @_when(flagged([SIDE.get(a + step) == a for a in planes]))
        def _():
            put(me, cpeer, side_send.at[(step + 1) // 2]).wait_send()

    put(me, cpeer, own_send.at[3]).wait_send()

    @_when(flagged([bool(RELAY[a]) for a in planes]))
    def _():
        put(me, cpeer, relay_send.at[0]).wait_send()

    @pl.when(has_next)
    def _():
        up_f.wait_send()
        up_c.wait_send()

    @pl.when(has_prev)
    def _():
        down_f.wait_send()
        down_c.wait_send()

    share.wait_send()
    for copy in give:
        copy.wait_send()
    loads[6].wait()
    wloads[2].wait()

    attend([stage_peer(1), stage_peer(2)], window)
    for j in (1, 2):
        put(me, cpeer, late_send.at[j]).wait_send()
    mixed = acc[window, :] * (1.0 / l_ref[window, :])
    residual = src[...].astype(F32) + jnp.dot(
        mixed.astype(BF16), wvo[...], preferred_element_type=F32
    )
    res_ref[...] = residual[width : width + tokens]
    v = _rms(residual, cg_ref[...].reshape(1, channels))
    activated = 0.5 * v * (1.0 + jnp.tanh(0.5 * v))
    spot = lax.broadcasted_iota(jnp.int32, (total, 1), 0)
    start = jnp.where(has_prev, 0, width)
    stop = jnp.where(has_next, total, total - width)
    activated = jnp.where((spot >= start) & (spot < stop), activated, 0.0).astype(BF16)
    conv(activated, 2)
    column_of = lax.broadcasted_iota(jnp.int32, (tokens, 1), 0) % width
    left = jnp.where(column_of == 0, 0.0, pltpu.roll(cacc[0], 1, 0))
    right = jnp.where(column_of == width - 1, 0.0, pltpu.roll(cacc[2], tokens - 1, 0))
    out_ref[...] = (left + cacc[1] + right).astype(BF16)


def settle(residual, conv_out, residual_hbm, out_hbm, sem):
    copies = [
        pltpu.make_async_copy(residual, residual_hbm, sem.at[0]),
        pltpu.make_async_copy(conv_out, out_hbm, sem.at[1]),
    ]
    for copy in copies:
        copy.start()
    for copy in copies:
        copy.wait()


def shards(features, conv_cache, norm_gain, w_query, w_key, w_value, w_out, conv_gain, conv_weight):
    frames, rows, width, channels = features.shape
    cached = conv_cache.shape[0]
    tokens = rows * width
    total = tokens + 2 * width
    count = lax.axis_size("row")
    outer = count // INNER
    hbm = pl.BlockSpec(memory_space=pltpu.HBM)
    vmem = pl.BlockSpec(memory_space=pltpu.VMEM)
    dma = pltpu.SemaphoreType.DMA
    square = pltpu.VMEM((channels, channels), BF16)
    lead = [pltpu.VMEM((channels,), F32), pltpu.VMEM((channels,), F32), pltpu.VMEM((count, tokens, channels), BF16)]
    lead += [pltpu.VMEM((total, channels), BF16), pltpu.VMEM((cached, total, channels), BF16)]
    lead += [square, square, square, square]
    kernels = pltpu.VMEM(conv_weight.shape, BF16)
    summed = pltpu.VMEM((3, tokens, channels), F32)
    if outer == UNROLL:
        body = grid_kernel
        both = 2 * (tokens + width)
        lanes = 128
        scratch = lead + [
            square,
            kernels,
            pltpu.VMEM((both, channels), BF16),
            pltpu.VMEM((both, 1), F32),
            pltpu.VMEM((both, 1), F32),
            pltpu.VMEM((both, channels), F32),
            pltpu.VMEM((total, channels), BF16),
            pltpu.VMEM((total, lanes), F32),
            pltpu.VMEM((total, channels), BF16),
            pltpu.VMEM((total, lanes), F32),
            summed,
            dma((8,)),
            dma((3,)),
            dma((4,)),
            dma((4,)),
            dma((4,)),
            dma((1,)),
            dma((3,)),
            dma((2,)),
            dma((3,)),
            dma((count,)),
            dma((3,)),
            dma((3,)),
            pltpu.SemaphoreType.REGULAR((UNROLL + 3,)),
        ]
    else:
        body = ring
        scratch = lead + [
            kernels,
            pltpu.VMEM((total, channels), BF16),
            pltpu.VMEM((total, 1), F32),
            pltpu.VMEM((total, 1), F32),
            pltpu.VMEM((total, channels), F32),
            summed,
            dma((8,)),
            dma((3,)),
            dma((4,)),
            dma((4,)),
            dma((outer, HALVES)),
            dma((outer, HALVES)),
            dma((2, outer, HALVES)),
            dma((count, HALVES)),
        ]
    residual, conv_out = pl.pallas_call(
        functools.partial(body, count, width),
        out_shape=(
            jax.ShapeDtypeStruct((tokens, channels), F32),
            jax.ShapeDtypeStruct((tokens, channels), BF16),
        ),
        in_specs=[hbm] * 9,
        out_specs=(vmem, vmem),
        scratch_shapes=scratch,
        compiler_params=pltpu.CompilerParams(
            collective_id=0, has_side_effects=True, vmem_limit_bytes=48 << 20
        ),
    )(
        *(
            pltpu.with_memory_space_constraint(x, pltpu.HBM)
            for x in (
                features.reshape(tokens, channels),
                conv_cache.reshape(cached, tokens, channels),
                norm_gain,
                w_query,
                w_key,
                w_value,
                w_out,
                conv_gain,
                conv_weight,
            )
        )
    )
    residual, conv_out = pl.pallas_call(
        settle,
        out_shape=(
            jax.ShapeDtypeStruct((tokens, channels), F32),
            jax.ShapeDtypeStruct((tokens, channels), BF16),
        ),
        in_specs=[vmem, vmem],
        out_specs=(hbm, hbm),
        scratch_shapes=[dma((2,))],
    )(*(pltpu.with_memory_space_constraint(a, pltpu.VMEM) for a in (residual, conv_out)))
    return (
        residual.reshape(frames, rows, width, channels),
        conv_out.reshape(frames, rows, width, channels),
    )


def solution(mesh):
    placed = (
        P(None, ("clip", "row"), None, None),
        P(None, ("clip", "row"), None, None),
        P(),
        P(),
        P(),
        P(),
        P(),
        P(),
        P(),
    )
    return jax.shard_map(
        shards,
        mesh=mesh,
        in_specs=placed,
        out_specs=(P(None, ("clip", "row"), None, None), P(None, ("clip", "row"), None, None)),
        check_vma=False,
    )
```

```python
import functools
import math

import jax
import jax.numpy as jnp
from jax import lax
from jax.experimental import pallas as pl
from jax.experimental.pallas import tpu as pltpu
from jax.sharding import PartitionSpec as P

MESH = pl.DeviceIdType.MESH
F32 = jnp.float32
BF16 = jnp.bfloat16
INNER = 4
UNROLL = 4
HALVES = 1
ORDER = (3, 1, 2)
DIRECT = {0: (1, 2, 3), 1: (0, 2), 2: (0, 1, 3), 3: (0, 2)}
RELAY = {0: ((3, 1),), 1: (), 2: ((1, 3),), 3: ()}
SIDE = {0: 1, 1: 2, 2: 1, 3: 2}
ARRIVE = {0: (1, 3, 2), 1: (0, 2, 3), 2: (1, 0, 3), 3: (2, 0, 1)}


def _rms(v, gain):
    return v * lax.rsqrt(jnp.mean(v * v, axis=-1, keepdims=True) + 1e-06) * gain


def _flip(index, bits):
    bit = 1
    while bit <= bits:
        if bits & bit:
            index = index + bit - 2 * bit * ((index // bit) % 2)
        bit *= 2
    return index


def _when(cond):
    if isinstance(cond, bool):
        return (lambda f: f()) if cond else (lambda f: None)
    return pl.when(cond)


def _both(a, b):
    if isinstance(a, bool) and isinstance(b, bool):
        return a and b
    return jnp.logical_and(a, b)


def ring(
    count,
    width,
    feat_hbm,
    cache_hbm,
    ng_hbm,
    wq_hbm,
    wk_hbm,
    wv_hbm,
    wo_hbm,
    cg_hbm,
    cw_hbm,
    res_ref,
    out_ref,
    ng_ref,
    cg_ref,
    blocks,
    src,
    ext,
    wq,
    wk,
    wv,
    wo,
    cw,
    qs,
    m_ref,
    l_ref,
    acc,
    cacc,
    load_sem,
    cw_sem,
    halo_send,
    halo_recv,
    z_send,
    x_send,
    c_send,
    recv,
):
    outer = count // INNER
    tokens, channels = feat_hbm.shape
    total = tokens + 2 * width
    me = lax.axis_index("row")
    z = me // INNER
    xpeer = me - z * INNER
    pair = (xpeer // 2) % 2
    core = xpeer % 2
    xpeer = me + 2 - 4 * pair
    cpeer = me + 1 - 2 * core
    static = outer == UNROLL
    piece = tokens // HALVES

    def zpeer(step):
        if static:
            return _flip(z, step)
        return lax.rem(z + step, outer)

    def zfrom(step):
        if static:
            return _flip(z, step)
        return lax.rem(z - step + outer, outer)

    def loop(low, high, body):
        if static:
            for step in range(low, high):
                body(step)
        else:
            lax.fori_loop(low, high, lambda i, carry: (body(i), carry)[1], 0)

    has_prev = me > 0
    has_next = me < count - 1
    prev = jnp.maximum(me - 1, 0)
    after = jnp.minimum(me + 1, count - 1)

    own = pl.ds(width, tokens)
    loads = [
        pltpu.make_async_copy(feat_hbm, src.at[own], load_sem.at[0]),
        pltpu.make_async_copy(wq_hbm, wq, load_sem.at[1]),
        pltpu.make_async_copy(wk_hbm, wk, load_sem.at[2]),
        pltpu.make_async_copy(cache_hbm, ext.at[:, own], load_sem.at[3]),
        pltpu.make_async_copy(wv_hbm, wv, load_sem.at[4]),
        pltpu.make_async_copy(wo_hbm, wo, load_sem.at[5]),
        pltpu.make_async_copy(cg_hbm, cg_ref, load_sem.at[6]),
    ]
    gains = pltpu.make_async_copy(ng_hbm, ng_ref, load_sem.at[7])
    gains.start()
    wloads = [pltpu.make_async_copy(cw_hbm.at[t], cw.at[t], cw_sem.at[t]) for t in range(3)]
    for copy in loads[:4]:
        copy.start()
    for copy in wloads[:2]:
        copy.start()
    for copy in loads[4:]:
        copy.start()
    wloads[2].start()

    barrier = pltpu.get_barrier_semaphore()

    def greet(device):
        pl.semaphore_signal(barrier, inc=1, device_id={"row": device}, device_id_type=MESH)

    def greet_z(step):
        greet(zpeer(step) * INNER + 2 * pair + core)

    loop(1, outer, greet_z)
    greet(xpeer)
    greet(cpeer)

    greet(lax.rem(me + 1, count))
    greet(lax.rem(me + count - 1, count))
    pl.semaphore_wait(barrier, outer + 3)

    def halo(a, b, index, device):
        return pltpu.make_async_remote_copy(
            src_ref=a,
            dst_ref=b,
            send_sem=halo_send.at[index],
            recv_sem=halo_recv.at[index],
            device_id={"row": device},
            device_id_type=MESH,
        )

    first = pl.ds(0, width)
    last = pl.ds(tokens - width, width)
    low = pl.ds(0, width)
    high = pl.ds(width + tokens, width)
    up_f = halo(feat_hbm.at[last], src.at[low], 0, after)
    down_f = halo(feat_hbm.at[first], src.at[high], 1, prev)
    up_c = halo(cache_hbm.at[:, last], ext.at[:, low], 2, after)
    down_c = halo(cache_hbm.at[:, first], ext.at[:, high], 3, prev)

    @pl.when(has_next)
    def _():
        up_f.start()

    @pl.when(has_prev)
    def _():
        down_f.start()

    def put(ident, h, sem, device):
        part = blocks.at[ident, pl.ds(h * piece, piece)]
        return pltpu.make_async_remote_copy(
            src_ref=part,
            dst_ref=part,
            send_sem=sem,
            recv_sem=recv.at[ident, h],
            device_id={"row": device},
            device_id_type=MESH,
        )

    def at(zi, p, c):
        return zi * INNER + 2 * p + c

    def z_put(step, h):
        if static and step == 2:
            return put(at(zpeer(3), pair, core), h, z_send.at[2, h], at(zpeer(1), pair, core))
        return put(me, h, z_send.at[step, h], at(zpeer(step), pair, core))

    def x_put(step, h):
        return put(at(zfrom(step), pair, core), h, x_send.at[step, h], xpeer)

    def c_put(step, h, which):
        p = pair if which == 0 else 1 - pair
        return put(at(zfrom(step), p, core), h, c_send.at[which, step, h], cpeer)

    def arrived(ident, h):
        put(ident, h, z_send.at[0, h], cpeer).wait_recv()

    gains.wait()
    gain = ng_ref[...].reshape(1, channels)
    loads[0].wait()
    blocks[me] = _rms(src[own, :].astype(F32), gain).astype(BF16)
    opening = [s for s in ORDER if s != 2] if static else range(1, min(outer, 3))
    for s in opening:
        for h in range(HALVES):
            if s == opening[0] or not static:
                z_put(s, h).start()
            if s == opening[0]:
                x_put(0, h).start()
    for h in range(HALVES):
        c_put(0, h, 0).start()

    @pl.when(has_next)
    def _():
        up_c.start()

    @pl.when(has_prev)
    def _():
        down_c.start()

    zero = jnp.zeros((width, channels), BF16)

    @pl.when(has_prev)
    def _():
        up_f.wait_recv()

    @pl.when(jnp.logical_not(has_prev))
    def _():
        src[low, :] = zero
        for t in range(ext.shape[0]):
            ext[t, low, :] = zero

    @pl.when(has_next)
    def _():
        down_f.wait_recv()

    @pl.when(jnp.logical_not(has_next))
    def _():
        src[high, :] = zero
        for t in range(ext.shape[0]):
            ext[t, high, :] = zero

    if static:
        z_put(opening[0], 0).wait_send()
        z_put(opening[1], 0).start()
    loads[1].wait()
    loads[2].wait()
    normed = _rms(src[...].astype(F32), gain).astype(BF16)
    query = jnp.dot(normed, wq[...], preferred_element_type=F32).astype(BF16)
    folded = lax.dot_general(
        query, wk[...], (((1,), (1,)), ((), ())), preferred_element_type=F32
    )
    qs[...] = (folded * (channels**-0.5 * math.log2(math.e))).astype(BF16)
    m_ref[...] = jnp.full(m_ref.shape, -1e30, F32)
    l_ref[...] = jnp.zeros(l_ref.shape, F32)
    acc[...] = jnp.zeros(acc.shape, F32)

    def conv(frame, t):
        taps = jnp.concatenate(
            [frame[dy * width : dy * width + tokens] for dy in range(3)], axis=-1
        )
        for dx in range(3):
            part = jnp.dot(
                taps,
                cw[t, :, dx].reshape(3 * channels, channels),
                preferred_element_type=F32,
            )
            if t == 0:
                cacc[dx] = part
            else:
                cacc[dx] += part

    def attend(step):
        zi = zfrom(step)
        keys = blocks[pl.ds(zi * INNER, INNER)].reshape(INNER * tokens, channels)
        scores = lax.dot_general(
            qs[...], keys, (((1,), (1,)), ((), ())), preferred_element_type=F32
        )
        old = m_ref[...]
        new = jnp.maximum(old, jnp.max(scores, axis=-1, keepdims=True))
        scale = jnp.exp2(old - new)
        expw = jnp.exp2(scores - new)
        m_ref[...] = new
        l_ref[...] = l_ref[...] * scale + jnp.sum(expw, axis=-1, keepdims=True)
        acc[...] = acc[...] * scale + jnp.dot(
            expw.astype(BF16), keys, preferred_element_type=F32
        )

    def stage_z(step, h):
        if not static:
            z_put(step, h).wait_send()

            @pl.when(step + 2 < outer)
            def _():
                z_put(step + 2, h).start()

        arrived(at(zfrom(step), pair, core), h)
        if static and step == 3:
            z_put(2, h).start()
        x_put(step, h).start()
        c_put(step, h, 0).start()

    def stage_x(step, h):
        arrived(at(zfrom(step), 1 - pair, core), h)
        c_put(step, h, 1).start()

    def stage_c(step, h):
        zi = zfrom(step)
        arrived(at(zi, pair, 1 - core), h)
        arrived(at(zi, 1 - pair, 1 - core), h)
        if h == HALVES - 1:
            attend(step)

    loads[3].wait()

    @pl.when(has_prev)
    def _():
        up_c.wait_recv()

    @pl.when(has_next)
    def _():
        down_c.wait_recv()

    if static:
        zunits = [(s, h) for s in ORDER for h in range(HALVES)]
        units = [(0, h) for h in range(HALVES)] + zunits
        for i in range(len(units) + 1):
            if i < len(zunits):
                stage_z(*zunits[i])
            if i < len(units):
                stage_x(*units[i])
            if i < 2:
                wloads[i].wait()
                conv(ext[i], i)
            if i > 0:
                stage_c(*units[i - 1])
    else:
        pieces = range(HALVES)
        for t in range(2):
            wloads[t].wait()
            conv(ext[t], t)
        for h in pieces:
            stage_x(0, h)
        for h in pieces:
            stage_z(1, h)

        def body(step):
            for h in pieces:
                stage_z(step, h)
            for h in pieces:
                stage_x(step - 1, h)
            for h in pieces:
                stage_c(step - 2, h)

        loop(2, outer, body)
        for h in pieces:
            stage_x(outer - 1, h)
        for s in (outer - 2, outer - 1):
            for h in pieces:
                stage_c(s, h)

    loads[4].wait()
    loads[5].wait()
    loads[6].wait()
    mixed = (acc[...] / l_ref[...]).astype(BF16)
    attended = jnp.dot(mixed, wv[...], preferred_element_type=F32).astype(BF16)
    residual = src[...].astype(F32) + jnp.dot(attended, wo[...], preferred_element_type=F32)
    res_ref[...] = residual[width : width + tokens]
    v = _rms(residual, cg_ref[...].reshape(1, channels))
    activated = v / (1.0 + jnp.exp(-v))
    spot = lax.broadcasted_iota(jnp.int32, (total, 1), 0)
    start = jnp.where(has_prev, 0, width)
    stop = jnp.where(has_next, total, total - width)
    activated = jnp.where((spot >= start) & (spot < stop), activated, 0.0).astype(BF16)
    wloads[2].wait()
    conv(activated, 2)
    column = lax.broadcasted_iota(jnp.int32, (tokens, 1), 0) % width
    left = jnp.where(column == 0, 0.0, pltpu.roll(cacc[0], 1, 0))
    right = jnp.where(column == width - 1, 0.0, pltpu.roll(cacc[2], tokens - 1, 0))
    out_ref[...] = (left + cacc[1] + right).astype(BF16)

    for h in range(HALVES):
        if static:
            for s in (opening[1], 2):
                z_put(s, h).wait_send()
        loop(0, outer, lambda s: x_put(s, h).wait_send())
        loop(0, outer, lambda s: c_put(s, h, 0).wait_send())
        loop(0, outer, lambda s: c_put(s, h, 1).wait_send())

    @pl.when(has_next)
    def _():
        up_f.wait_send()
        up_c.wait_send()

    @pl.when(has_prev)
    def _():
        down_f.wait_send()
        down_c.wait_send()


def among(z, values):
    if all(v == values[0] for v in values):
        return values[0]
    out = values[-1]
    for i in range(len(values) - 1):
        out = jnp.where(z == i, values[i], out)
    return out


def column_plan():
    flips = {}
    for z in range(UNROLL):
        for q in range(UNROLL):
            relayed = any((q, z) in RELAY[a] for a in range(UNROLL))
            flips[z, q] = 0 if relayed else 1
    sends = {(a, b) for a in range(UNROLL) for b in DIRECT[a]}
    sends |= {(a, d) for a in range(UNROLL) for _, d in RELAY[a]}
    return flips, sends


def grid_kernel(
    count,
    width,
    feat_hbm,
    cache_hbm,
    ng_hbm,
    wq_hbm,
    wk_hbm,
    wv_hbm,
    wo_hbm,
    cg_hbm,
    cw_hbm,
    res_ref,
    out_ref,
    ng_ref,
    cg_ref,
    blocks,
    src,
    ext,
    wq,
    wk,
    wv,
    wo,
    wvo,
    cw,
    qs,
    m_ref,
    l_ref,
    acc,
    part_acc,
    part_ml,
    peer_acc,
    peer_ml,
    cacc,
    load_sem,
    cw_sem,
    halo_send,
    halo_recv,
    own_send,
    relay_send,
    x_send,
    side_send,
    late_send,
    recv,
    pair_send,
    pair_recv,
    reply,
):
    tokens, channels = feat_hbm.shape
    total = tokens + 2 * width
    half = tokens + width
    me = lax.axis_index("row")
    z = me // INNER
    x = (me // 2) % 2
    c = me % 2
    flips, sends = column_plan()
    planes = range(UNROLL)

    def at(zi, xi, ci):
        return zi * INNER + 2 * xi + ci

    xpeer = at(z, 1 - x, 1 - c)
    cpeer = at(z, x, 1 - c)
    has_prev = me > 0
    has_next = me < count - 1
    prev = jnp.maximum(me - 1, 0)
    after = jnp.minimum(me + 1, count - 1)
    down_plane = (x == 0) & (c == 0) & (z > 0)
    up_plane = (x == 1) & (c == 1) & (z < UNROLL - 1)

    def flagged(values):
        chosen = among(z, [int(v) for v in values])
        return bool(chosen) if isinstance(chosen, int) else chosen == 1

    def signal(sem, device):
        pl.semaphore_signal(sem, inc=1, device_id={"row": device}, device_id_type=MESH)

    def partners(a, b):
        return (a, b) in sends or (b, a) in sends

    barrier = pltpu.get_barrier_semaphore()
    for q in planes:
        @_when(flagged([q > a and partners(a, q) for a in planes]))
        def _():
            signal(barrier, at(q, x, 1 - c))

    @pl.when(x == 0)
    def _():
        signal(barrier, xpeer)

    @pl.when(c == 0)
    def _():
        signal(barrier, cpeer)

    @pl.when(up_plane)
    def _():
        signal(barrier, after)

    own = pl.ds(width, tokens)
    loads = [
        pltpu.make_async_copy(feat_hbm, src.at[own], load_sem.at[0]),
        pltpu.make_async_copy(wq_hbm, wq, load_sem.at[1]),
        pltpu.make_async_copy(wk_hbm, wk, load_sem.at[2]),
        pltpu.make_async_copy(cache_hbm, ext.at[:, own], load_sem.at[3]),
        pltpu.make_async_copy(wv_hbm, wv, load_sem.at[4]),
        pltpu.make_async_copy(wo_hbm, wo, load_sem.at[5]),
        pltpu.make_async_copy(cg_hbm, cg_ref, load_sem.at[6]),
        pltpu.make_async_copy(ng_hbm, ng_ref, load_sem.at[7]),
    ]
    wloads = [pltpu.make_async_copy(cw_hbm.at[t], cw.at[t], cw_sem.at[t]) for t in range(3)]
    loads[0].start()
    loads[7].start()

    lower = among(z, [sum(partners(q, a) for q in range(a)) for a in planes])

    @pl.when(me > 0)
    def _():
        pl.semaphore_wait(barrier, lower + x + c + jnp.where(down_plane, 1, 0))

    for q in planes[:-1]:
        @_when(flagged([q < a and (q, a) in sends for a in planes]))
        def _():
            signal(reply.at[z], at(q, x, 1 - c))

    @pl.when(x == 1)
    def _():
        signal(reply.at[UNROLL], xpeer)

    @pl.when(c == 1)
    def _():
        signal(reply.at[UNROLL + 1], cpeer)

    @pl.when(down_plane)
    def _():
        signal(reply.at[UNROLL + 2], prev)

    for copy in (loads[1], loads[2], loads[4], loads[5], loads[3], wloads[0], wloads[1], loads[6], wloads[2]):
        copy.start()

    def remote(a, b, send, receive, device):
        return pltpu.make_async_remote_copy(
            src_ref=a,
            dst_ref=b,
            send_sem=send,
            recv_sem=receive,
            device_id={"row": device},
            device_id_type=MESH,
        )

    def halo(a, b, index, device):
        return remote(a, b, halo_send.at[index], halo_recv.at[index], device)

    first = pl.ds(0, width)
    last = pl.ds(tokens - width, width)
    low = pl.ds(0, width)
    high = pl.ds(width + tokens, width)
    up_f = halo(feat_hbm.at[last], src.at[low], 0, after)
    down_f = halo(feat_hbm.at[first], src.at[high], 1, prev)
    up_c = halo(cache_hbm.at[:, last], ext.at[:, low], 2, after)
    down_c = halo(cache_hbm.at[:, first], ext.at[:, high], 3, prev)

    def put(ident, device, sem):
        part = blocks.at[ident]
        return remote(part, part, sem, recv.at[ident], device)

    def z_send(j):
        dest = among(z, [DIRECT[a][j] if j < len(DIRECT[a]) else 0 for a in planes])

        @_when(flagged([j < len(DIRECT[a]) for a in planes]))
        def _():
            @pl.when(dest > z)
            def _():
                pl.semaphore_wait(reply.at[dest], 1)

            put(me, at(dest, x, 1 - c), own_send.at[j]).start()

    def x_own():
        @pl.when(x == 0)
        def _():
            pl.semaphore_wait(reply.at[UNROLL], 1)

        put(me, xpeer, own_send.at[3]).start()

    def arrived(ident):
        put(ident, cpeer, own_send.at[0]).wait_recv()

    loads[0].wait()
    loads[7].wait()
    gain = ng_ref[...].reshape(1, channels)
    blocks[me] = _rms(src[own, :].astype(F32), gain).astype(BF16)
    z_send(0)
    x_own()
    z_send(1)

    @pl.when(c == 0)
    def _():
        pl.semaphore_wait(reply.at[UNROLL + 1], 1)

    @pl.when(up_plane)
    def _():
        pl.semaphore_wait(reply.at[UNROLL + 2], 1)

    @pl.when(has_next)
    def _():
        up_f.start()

    @pl.when(has_prev)
    def _():
        down_f.start()

    @pl.when(has_next)
    def _():
        up_c.start()

    @pl.when(has_prev)
    def _():
        down_c.start()

    z_send(2)

    zero = jnp.zeros((width, channels), BF16)

    @pl.when(jnp.logical_not(has_prev))
    def _():
        src[low, :] = zero
        for t in range(ext.shape[0]):
            ext[t, low, :] = zero

    @pl.when(jnp.logical_not(has_next))
    def _():
        src[high, :] = zero
        for t in range(ext.shape[0]):
            ext[t, high, :] = zero

    def conv(frame, t):
        taps = jnp.concatenate(
            [frame[dy * width : dy * width + tokens] for dy in range(3)], axis=-1
        )
        sums = []
        for dx in range(3):
            part = jnp.dot(
                taps,
                cw[t, :, dx].reshape(3 * channels, channels),
                preferred_element_type=F32,
            )
            if t == 0:
                cacc[dx] = part
            elif t == 1:
                cacc[dx] += part
            else:
                sums.append(cacc[dx] + part)
        return sums

    def attend(idents, rows=slice(None), opening=False):
        keys = jnp.concatenate([blocks[u] for u in idents], axis=0)
        scores = lax.dot_general(
            qs[rows, :], keys, (((1,), (1,)), ((), ())), preferred_element_type=F32
        )
        peak = jnp.max(scores, axis=-1, keepdims=True)
        if opening:
            new = peak
        else:
            old = m_ref[rows, :]
            new = jnp.maximum(old, peak)
            scale = jnp.exp2(old - new)
        expw = jnp.exp2(scores - new)
        m_ref[rows, :] = new
        mass = jnp.sum(expw, axis=-1, keepdims=True)
        value = jnp.dot(expw.astype(BF16), keys, preferred_element_type=F32)
        if opening:
            l_ref[rows, :] = mass
            acc[rows, :] = value
        else:
            l_ref[rows, :] = l_ref[rows, :] * scale + mass
            acc[rows, :] = acc[rows, :] * scale + value

    def column(j):
        q = among(z, [ARRIVE[a][j] for a in planes])
        flip = among(z, [flips[a, ARRIVE[a][j]] for a in planes])
        return q, c + flip - 2 * c * flip

    def stage_z(j):
        q, core = column(j)
        ident = at(q, x, core)
        arrived(ident)
        if any(RELAY.values()):
            relayed = among(z, [RELAY[a][0][0] if RELAY[a] else UNROLL for a in planes])
            dest = among(z, [RELAY[a][0][1] if RELAY[a] else 0 for a in planes])

            @pl.when(q == relayed)
            def _():
                put(ident, at(dest, x, 1 - c), relay_send.at[0]).start()

        @_when(flagged([ARRIVE[a][j] != SIDE[a] for a in planes]))
        def _():
            put(ident, xpeer, x_send.at[j]).start()

        return ident

    def stage_side():
        arrived(xpeer)
        for step in (-1, 1):
            @_when(flagged([SIDE.get(a + step) == a for a in planes]))
            def _():
                put(xpeer, at(z + step, x, 1 - c), side_send.at[(step + 1) // 2]).start()

    def stage_x(j):
        q, core = column(j)
        ident = at(q, 1 - x, 1 - core)
        arrived(ident)
        return ident

    def stage_late(j):
        ident = stage_x(j)
        put(ident, cpeer, late_send.at[j]).start()
        return ident

    def stage_peer(j):
        q, core = column(j)
        ident = at(q, 1 - x, core)
        arrived(ident)
        return ident

    loads[4].wait()
    loads[5].wait()
    wvo[...] = jnp.dot(wv[...], wo[...], preferred_element_type=F32).astype(BF16)
    z0 = stage_z(0)
    stage_side()
    z1 = stage_z(1)
    @pl.when(has_prev)
    def _():
        up_f.wait_recv()

    @pl.when(has_next)
    def _():
        down_f.wait_recv()

    loads[1].wait()
    loads[2].wait()
    mine = pl.ds(pl.multiple_of(c * half, 16), half)
    rows = src[pl.ds(pl.multiple_of(c * width, 16), half), :].astype(F32)
    query = jnp.dot(_rms(rows, gain).astype(BF16), wq[...], preferred_element_type=F32).astype(BF16)
    folded = lax.dot_general(
        query, wk[...], (((1,), (1,)), ((), ())), preferred_element_type=F32
    )
    qs[mine, :] = (folded * (channels**-0.5 * math.log2(math.e))).astype(BF16)
    share = remote(qs.at[mine], qs.at[mine], pair_send.at[0], pair_recv.at[0], cpeer)
    share.start()
    z2 = stage_z(2)
    share.wait_recv()
    attend([me, xpeer, z0, z1], opening=True)
    loads[3].wait()

    @pl.when(has_prev)
    def _():
        up_c.wait_recv()

    @pl.when(has_next)
    def _():
        down_c.wait_recv()

    wloads[0].wait()
    conv(ext[0], 0)
    x0 = stage_x(0)
    attend([z2, x0])
    theirs = pl.ds(pl.multiple_of((1 - c) * tokens, 16), total)
    window = pl.ds(pl.multiple_of(c * tokens, 16), total)
    part_acc[...] = acc[theirs, :].astype(BF16)
    lane = lax.broadcasted_iota(jnp.int32, part_ml.shape, 1)
    part_ml[...] = jnp.where(lane < part_ml.shape[1] // 2, m_ref[theirs, :], l_ref[theirs, :])
    give = [
        remote(part_acc, peer_acc, pair_send.at[1], pair_recv.at[1], cpeer),
        remote(part_ml, peer_ml, pair_send.at[2], pair_recv.at[2], cpeer),
    ]
    for copy in give:
        copy.start()

    def merge():
        for copy in give:
            copy.wait_recv()
        peer_m = peer_ml[:, :1]
        peer_l = peer_ml[:, part_ml.shape[1] // 2 :][:, :1]
        own_m = m_ref[window, :]
        new = jnp.maximum(own_m, peer_m)
        own_w = jnp.exp2(own_m - new)
        peer_w = jnp.exp2(peer_m - new)
        m_ref[window, :] = new
        l_ref[window, :] = l_ref[window, :] * own_w + peer_l * peer_w
        acc[window, :] = acc[window, :] * own_w + peer_acc[...].astype(F32) * peer_w

    wloads[1].wait()
    conv(ext[1], 1)
    x1 = stage_late(1)
    x2 = stage_late(2)
    merge()
    attend([x1, x2], window)
    for j in range(3):
        @_when(flagged([j < len(DIRECT[a]) for a in planes]))
        def _():
            put(me, cpeer, own_send.at[j]).wait_send()

        @_when(flagged([ARRIVE[a][j] != SIDE[a] for a in planes]))
        def _():
            put(me, cpeer, x_send.at[j]).wait_send()

    for step in (-1, 1):
        @_when(flagged([SIDE.get(a + step) == a for a in planes]))
        def _():
            put(me, cpeer, side_send.at[(step + 1) // 2]).wait_send()

    put(me, cpeer, own_send.at[3]).wait_send()

    @_when(flagged([bool(RELAY[a]) for a in planes]))
    def _():
        put(me, cpeer, relay_send.at[0]).wait_send()

    @pl.when(has_next)
    def _():
        up_f.wait_send()
        up_c.wait_send()

    @pl.when(has_prev)
    def _():
        down_f.wait_send()
        down_c.wait_send()

    share.wait_send()
    for copy in give:
        copy.wait_send()
    loads[6].wait()
    wloads[2].wait()

    attend([stage_peer(1), stage_peer(2)], window)
    for j in (1, 2):
        put(me, cpeer, late_send.at[j]).wait_send()
    mixed = acc[window, :] * (1.0 / l_ref[window, :])
    residual = src[...].astype(F32) + jnp.dot(
        mixed.astype(BF16), wvo[...], preferred_element_type=F32
    )
    res_ref[...] = residual[width : width + tokens]
    v = _rms(residual, cg_ref[...].reshape(1, channels))
    activated = 0.5 * v * (1.0 + jnp.tanh(0.5 * v))
    spot = lax.broadcasted_iota(jnp.int32, (total, 1), 0)
    start = jnp.where(has_prev, 0, width)
    stop = jnp.where(has_next, total, total - width)
    activated = jnp.where((spot >= start) & (spot < stop), activated, 0.0).astype(BF16)
    sums = conv(activated, 2)
    column_of = lax.broadcasted_iota(jnp.int32, (tokens, 1), 0) % width
    left = jnp.where(column_of == 0, 0.0, pltpu.roll(sums[0], 1, 0))
    right = jnp.where(column_of == width - 1, 0.0, pltpu.roll(sums[2], tokens - 1, 0))
    out_ref[...] = (left + sums[1] + right).astype(BF16)


def settle(residual, conv_out, residual_hbm, out_hbm, sem):
    copies = [
        pltpu.make_async_copy(residual, residual_hbm, sem.at[0]),
        pltpu.make_async_copy(conv_out, out_hbm, sem.at[1]),
    ]
    for copy in copies:
        copy.start()
    for copy in copies:
        copy.wait()


def shards(features, conv_cache, norm_gain, w_query, w_key, w_value, w_out, conv_gain, conv_weight):
    frames, rows, width, channels = features.shape
    cached = conv_cache.shape[0]
    tokens = rows * width
    total = tokens + 2 * width
    count = lax.axis_size("row")
    outer = count // INNER
    hbm = pl.BlockSpec(memory_space=pltpu.HBM)
    vmem = pl.BlockSpec(memory_space=pltpu.VMEM)
    dma = pltpu.SemaphoreType.DMA
    square = pltpu.VMEM((channels, channels), BF16)
    lead = [pltpu.VMEM((channels,), F32), pltpu.VMEM((channels,), F32), pltpu.VMEM((count, tokens, channels), BF16)]
    lead += [pltpu.VMEM((total, channels), BF16), pltpu.VMEM((cached, total, channels), BF16)]
    lead += [square, square, square, square]
    kernels = pltpu.VMEM(conv_weight.shape, BF16)
    summed = pltpu.VMEM((3, tokens, channels), F32)
    if outer == UNROLL:
        body = grid_kernel
        both = 2 * (tokens + width)
        lanes = 128
        scratch = lead + [
            square,
            kernels,
            pltpu.VMEM((both, channels), BF16),
            pltpu.VMEM((both, 1), F32),
            pltpu.VMEM((both, 1), F32),
            pltpu.VMEM((both, channels), F32),
            pltpu.VMEM((total, channels), BF16),
            pltpu.VMEM((total, lanes), F32),
            pltpu.VMEM((total, channels), BF16),
            pltpu.VMEM((total, lanes), F32),
            summed,
            dma((8,)),
            dma((3,)),
            dma((4,)),
            dma((4,)),
            dma((4,)),
            dma((1,)),
            dma((3,)),
            dma((2,)),
            dma((3,)),
            dma((count,)),
            dma((3,)),
            dma((3,)),
            pltpu.SemaphoreType.REGULAR((UNROLL + 3,)),
        ]
    else:
        body = ring
        scratch = lead + [
            kernels,
            pltpu.VMEM((total, channels), BF16),
            pltpu.VMEM((total, 1), F32),
            pltpu.VMEM((total, 1), F32),
            pltpu.VMEM((total, channels), F32),
            summed,
            dma((8,)),
            dma((3,)),
            dma((4,)),
            dma((4,)),
            dma((outer, HALVES)),
            dma((outer, HALVES)),
            dma((2, outer, HALVES)),
            dma((count, HALVES)),
        ]
    residual, conv_out = pl.pallas_call(
        functools.partial(body, count, width),
        out_shape=(
            jax.ShapeDtypeStruct((tokens, channels), F32),
            jax.ShapeDtypeStruct((tokens, channels), BF16),
        ),
        in_specs=[hbm] * 9,
        out_specs=(vmem, vmem),
        scratch_shapes=scratch,
        compiler_params=pltpu.CompilerParams(
            collective_id=0, has_side_effects=True, vmem_limit_bytes=48 << 20
        ),
    )(
        *(
            pltpu.with_memory_space_constraint(x, pltpu.HBM)
            for x in (
                features.reshape(tokens, channels),
                conv_cache.reshape(cached, tokens, channels),
                norm_gain,
                w_query,
                w_key,
                w_value,
                w_out,
                conv_gain,
                conv_weight,
            )
        )
    )
    residual, conv_out = pl.pallas_call(
        settle,
        out_shape=(
            jax.ShapeDtypeStruct((tokens, channels), F32),
            jax.ShapeDtypeStruct((tokens, channels), BF16),
        ),
        in_specs=[vmem, vmem],
        out_specs=(hbm, hbm),
        scratch_shapes=[dma((2,))],
    )(*(pltpu.with_memory_space_constraint(a, pltpu.VMEM) for a in (residual, conv_out)))
    return (
        residual.reshape(frames, rows, width, channels),
        conv_out.reshape(frames, rows, width, channels),
    )


def solution(mesh):
    placed = (
        P(None, ("clip", "row"), None, None),
        P(None, ("clip", "row"), None, None),
        P(),
        P(),
        P(),
        P(),
        P(),
        P(),
        P(),
    )
    return jax.shard_map(
        shards,
        mesh=mesh,
        in_specs=placed,
        out_specs=(P(None, ("clip", "row"), None, None), P(None, ("clip", "row"), None, None)),
        check_vma=False,
    )
```

```python
import functools
import math

import jax
import jax.numpy as jnp
from jax import lax
from jax.experimental import pallas as pl
from jax.experimental.pallas import tpu as pltpu
from jax.sharding import PartitionSpec as P

MESH = pl.DeviceIdType.MESH
F32 = jnp.float32
BF16 = jnp.bfloat16
INNER = 4
UNROLL = 4
HALVES = 1
ORDER = (3, 1, 2)
DIRECT = {0: (1, 2, 3), 1: (0, 2), 2: (0, 1, 3), 3: (0, 2)}
RELAY = {0: ((3, 1),), 1: (), 2: ((1, 3),), 3: ()}
SIDE = {0: 1, 1: 2, 2: 1, 3: 2}
ARRIVE = {0: (1, 3, 2), 1: (0, 2, 3), 2: (1, 0, 3), 3: (2, 0, 1)}


def _rms(v, gain):
    return v * lax.rsqrt(jnp.mean(v * v, axis=-1, keepdims=True) + 1e-06) * gain


def _flip(index, bits):
    bit = 1
    while bit <= bits:
        if bits & bit:
            index = index + bit - 2 * bit * ((index // bit) % 2)
        bit *= 2
    return index


def _when(cond):
    if isinstance(cond, bool):
        return (lambda f: f()) if cond else (lambda f: None)
    return pl.when(cond)


def _both(a, b):
    if isinstance(a, bool) and isinstance(b, bool):
        return a and b
    return jnp.logical_and(a, b)


def ring(
    count,
    width,
    feat_hbm,
    cache_hbm,
    ng_hbm,
    wq_hbm,
    wk_hbm,
    wv_hbm,
    wo_hbm,
    cg_hbm,
    cw_hbm,
    res_ref,
    out_ref,
    ng_ref,
    cg_ref,
    blocks,
    src,
    ext,
    wq,
    wk,
    wv,
    wo,
    cw,
    qs,
    m_ref,
    l_ref,
    acc,
    cacc,
    load_sem,
    cw_sem,
    halo_send,
    halo_recv,
    z_send,
    x_send,
    c_send,
    recv,
):
    outer = count // INNER
    tokens, channels = feat_hbm.shape
    total = tokens + 2 * width
    me = lax.axis_index("row")
    z = me // INNER
    xpeer = me - z * INNER
    pair = (xpeer // 2) % 2
    core = xpeer % 2
    xpeer = me + 2 - 4 * pair
    cpeer = me + 1 - 2 * core
    static = outer == UNROLL
    piece = tokens // HALVES

    def zpeer(step):
        if static:
            return _flip(z, step)
        return lax.rem(z + step, outer)

    def zfrom(step):
        if static:
            return _flip(z, step)
        return lax.rem(z - step + outer, outer)

    def loop(low, high, body):
        if static:
            for step in range(low, high):
                body(step)
        else:
            lax.fori_loop(low, high, lambda i, carry: (body(i), carry)[1], 0)

    has_prev = me > 0
    has_next = me < count - 1
    prev = jnp.maximum(me - 1, 0)
    after = jnp.minimum(me + 1, count - 1)

    own = pl.ds(width, tokens)
    loads = [
        pltpu.make_async_copy(feat_hbm, src.at[own], load_sem.at[0]),
        pltpu.make_async_copy(wq_hbm, wq, load_sem.at[1]),
        pltpu.make_async_copy(wk_hbm, wk, load_sem.at[2]),
        pltpu.make_async_copy(cache_hbm, ext.at[:, own], load_sem.at[3]),
        pltpu.make_async_copy(wv_hbm, wv, load_sem.at[4]),
        pltpu.make_async_copy(wo_hbm, wo, load_sem.at[5]),
        pltpu.make_async_copy(cg_hbm, cg_ref, load_sem.at[6]),
    ]
    gains = pltpu.make_async_copy(ng_hbm, ng_ref, load_sem.at[7])
    gains.start()
    wloads = [pltpu.make_async_copy(cw_hbm.at[t], cw.at[t], cw_sem.at[t]) for t in range(3)]
    for copy in loads[:4]:
        copy.start()
    for copy in wloads[:2]:
        copy.start()
    for copy in loads[4:]:
        copy.start()
    wloads[2].start()

    barrier = pltpu.get_barrier_semaphore()

    def greet(device):
        pl.semaphore_signal(barrier, inc=1, device_id={"row": device}, device_id_type=MESH)

    def greet_z(step):
        greet(zpeer(step) * INNER + 2 * pair + core)

    loop(1, outer, greet_z)
    greet(xpeer)
    greet(cpeer)

    greet(lax.rem(me + 1, count))
    greet(lax.rem(me + count - 1, count))
    pl.semaphore_wait(barrier, outer + 3)

    def halo(a, b, index, device):
        return pltpu.make_async_remote_copy(
            src_ref=a,
            dst_ref=b,
            send_sem=halo_send.at[index],
            recv_sem=halo_recv.at[index],
            device_id={"row": device},
            device_id_type=MESH,
        )

    first = pl.ds(0, width)
    last = pl.ds(tokens - width, width)
    low = pl.ds(0, width)
    high = pl.ds(width + tokens, width)
    up_f = halo(feat_hbm.at[last], src.at[low], 0, after)
    down_f = halo(feat_hbm.at[first], src.at[high], 1, prev)
    up_c = halo(cache_hbm.at[:, last], ext.at[:, low], 2, after)
    down_c = halo(cache_hbm.at[:, first], ext.at[:, high], 3, prev)

    @pl.when(has_next)
    def _():
        up_f.start()

    @pl.when(has_prev)
    def _():
        down_f.start()

    def put(ident, h, sem, device):
        part = blocks.at[ident, pl.ds(h * piece, piece)]
        return pltpu.make_async_remote_copy(
            src_ref=part,
            dst_ref=part,
            send_sem=sem,
            recv_sem=recv.at[ident, h],
            device_id={"row": device},
            device_id_type=MESH,
        )

    def at(zi, p, c):
        return zi * INNER + 2 * p + c

    def z_put(step, h):
        if static and step == 2:
            return put(at(zpeer(3), pair, core), h, z_send.at[2, h], at(zpeer(1), pair, core))
        return put(me, h, z_send.at[step, h], at(zpeer(step), pair, core))

    def x_put(step, h):
        return put(at(zfrom(step), pair, core), h, x_send.at[step, h], xpeer)

    def c_put(step, h, which):
        p = pair if which == 0 else 1 - pair
        return put(at(zfrom(step), p, core), h, c_send.at[which, step, h], cpeer)

    def arrived(ident, h):
        put(ident, h, z_send.at[0, h], cpeer).wait_recv()

    gains.wait()
    gain = ng_ref[...].reshape(1, channels)
    loads[0].wait()
    blocks[me] = _rms(src[own, :].astype(F32), gain).astype(BF16)
    opening = [s for s in ORDER if s != 2] if static else range(1, min(outer, 3))
    for s in opening:
        for h in range(HALVES):
            if s == opening[0] or not static:
                z_put(s, h).start()
            if s == opening[0]:
                x_put(0, h).start()
    for h in range(HALVES):
        c_put(0, h, 0).start()

    @pl.when(has_next)
    def _():
        up_c.start()

    @pl.when(has_prev)
    def _():
        down_c.start()

    zero = jnp.zeros((width, channels), BF16)

    @pl.when(has_prev)
    def _():
        up_f.wait_recv()

    @pl.when(jnp.logical_not(has_prev))
    def _():
        src[low, :] = zero
        for t in range(ext.shape[0]):
            ext[t, low, :] = zero

    @pl.when(has_next)
    def _():
        down_f.wait_recv()

    @pl.when(jnp.logical_not(has_next))
    def _():
        src[high, :] = zero
        for t in range(ext.shape[0]):
            ext[t, high, :] = zero

    if static:
        z_put(opening[0], 0).wait_send()
        z_put(opening[1], 0).start()
    loads[1].wait()
    loads[2].wait()
    normed = _rms(src[...].astype(F32), gain).astype(BF16)
    query = jnp.dot(normed, wq[...], preferred_element_type=F32).astype(BF16)
    folded = lax.dot_general(
        query, wk[...], (((1,), (1,)), ((), ())), preferred_element_type=F32
    )
    qs[...] = (folded * (channels**-0.5 * math.log2(math.e))).astype(BF16)
    m_ref[...] = jnp.full(m_ref.shape, -1e30, F32)
    l_ref[...] = jnp.zeros(l_ref.shape, F32)
    acc[...] = jnp.zeros(acc.shape, F32)

    def conv(frame, t):
        taps = jnp.concatenate(
            [frame[dy * width : dy * width + tokens] for dy in range(3)], axis=-1
        )
        for dx in range(3):
            part = jnp.dot(
                taps,
                cw[t, :, dx].reshape(3 * channels, channels),
                preferred_element_type=F32,
            )
            if t == 0:
                cacc[dx] = part
            else:
                cacc[dx] += part

    def attend(step):
        zi = zfrom(step)
        keys = blocks[pl.ds(zi * INNER, INNER)].reshape(INNER * tokens, channels)
        scores = lax.dot_general(
            qs[...], keys, (((1,), (1,)), ((), ())), preferred_element_type=F32
        )
        old = m_ref[...]
        new = jnp.maximum(old, jnp.max(scores, axis=-1, keepdims=True))
        scale = jnp.exp2(old - new)
        expw = jnp.exp2(scores - new)
        m_ref[...] = new
        l_ref[...] = l_ref[...] * scale + jnp.sum(expw, axis=-1, keepdims=True)
        acc[...] = acc[...] * scale + jnp.dot(
            expw.astype(BF16), keys, preferred_element_type=F32
        )

    def stage_z(step, h):
        if not static:
            z_put(step, h).wait_send()

            @pl.when(step + 2 < outer)
            def _():
                z_put(step + 2, h).start()

        arrived(at(zfrom(step), pair, core), h)
        if static and step == 3:
            z_put(2, h).start()
        x_put(step, h).start()
        c_put(step, h, 0).start()

    def stage_x(step, h):
        arrived(at(zfrom(step), 1 - pair, core), h)
        c_put(step, h, 1).start()

    def stage_c(step, h):
        zi = zfrom(step)
        arrived(at(zi, pair, 1 - core), h)
        arrived(at(zi, 1 - pair, 1 - core), h)
        if h == HALVES - 1:
            attend(step)

    loads[3].wait()

    @pl.when(has_prev)
    def _():
        up_c.wait_recv()

    @pl.when(has_next)
    def _():
        down_c.wait_recv()

    if static:
        zunits = [(s, h) for s in ORDER for h in range(HALVES)]
        units = [(0, h) for h in range(HALVES)] + zunits
        for i in range(len(units) + 1):
            if i < len(zunits):
                stage_z(*zunits[i])
            if i < len(units):
                stage_x(*units[i])
            if i < 2:
                wloads[i].wait()
                conv(ext[i], i)
            if i > 0:
                stage_c(*units[i - 1])
    else:
        pieces = range(HALVES)
        for t in range(2):
            wloads[t].wait()
            conv(ext[t], t)
        for h in pieces:
            stage_x(0, h)
        for h in pieces:
            stage_z(1, h)

        def body(step):
            for h in pieces:
                stage_z(step, h)
            for h in pieces:
                stage_x(step - 1, h)
            for h in pieces:
                stage_c(step - 2, h)

        loop(2, outer, body)
        for h in pieces:
            stage_x(outer - 1, h)
        for s in (outer - 2, outer - 1):
            for h in pieces:
                stage_c(s, h)

    loads[4].wait()
    loads[5].wait()
    loads[6].wait()
    mixed = (acc[...] / l_ref[...]).astype(BF16)
    attended = jnp.dot(mixed, wv[...], preferred_element_type=F32).astype(BF16)
    residual = src[...].astype(F32) + jnp.dot(attended, wo[...], preferred_element_type=F32)
    res_ref[...] = residual[width : width + tokens]
    v = _rms(residual, cg_ref[...].reshape(1, channels))
    activated = v / (1.0 + jnp.exp(-v))
    spot = lax.broadcasted_iota(jnp.int32, (total, 1), 0)
    start = jnp.where(has_prev, 0, width)
    stop = jnp.where(has_next, total, total - width)
    activated = jnp.where((spot >= start) & (spot < stop), activated, 0.0).astype(BF16)
    wloads[2].wait()
    conv(activated, 2)
    column = lax.broadcasted_iota(jnp.int32, (tokens, 1), 0) % width
    left = jnp.where(column == 0, 0.0, pltpu.roll(cacc[0], 1, 0))
    right = jnp.where(column == width - 1, 0.0, pltpu.roll(cacc[2], tokens - 1, 0))
    out_ref[...] = (left + cacc[1] + right).astype(BF16)

    for h in range(HALVES):
        if static:
            for s in (opening[1], 2):
                z_put(s, h).wait_send()
        loop(0, outer, lambda s: x_put(s, h).wait_send())
        loop(0, outer, lambda s: c_put(s, h, 0).wait_send())
        loop(0, outer, lambda s: c_put(s, h, 1).wait_send())

    @pl.when(has_next)
    def _():
        up_f.wait_send()
        up_c.wait_send()

    @pl.when(has_prev)
    def _():
        down_f.wait_send()
        down_c.wait_send()


def among(z, values):
    if all(v == values[0] for v in values):
        return values[0]
    out = values[-1]
    for i in range(len(values) - 1):
        out = jnp.where(z == i, values[i], out)
    return out


def column_plan():
    flips = {}
    for z in range(UNROLL):
        for q in range(UNROLL):
            relayed = any((q, z) in RELAY[a] for a in range(UNROLL))
            flips[z, q] = 0 if relayed else 1
    sends = {(a, b) for a in range(UNROLL) for b in DIRECT[a]}
    sends |= {(a, d) for a in range(UNROLL) for _, d in RELAY[a]}
    return flips, sends


def grid_kernel(
    count,
    width,
    feat_hbm,
    cache_hbm,
    ng_hbm,
    wq_hbm,
    wk_hbm,
    wv_hbm,
    wo_hbm,
    cg_hbm,
    cw_hbm,
    res_ref,
    out_ref,
    ng_ref,
    cg_ref,
    blocks,
    src,
    ext,
    wq,
    wk,
    wv,
    wo,
    wvo,
    cw,
    qs,
    m_ref,
    l_ref,
    acc,
    part_acc,
    part_ml,
    peer_acc,
    peer_ml,
    cacc,
    load_sem,
    cw_sem,
    halo_send,
    halo_recv,
    own_send,
    relay_send,
    x_send,
    side_send,
    late_send,
    recv,
    pair_send,
    pair_recv,
    reply,
):
    tokens, channels = feat_hbm.shape
    total = tokens + 2 * width
    half = tokens + width
    me = lax.axis_index("row")
    z = me // INNER
    x = (me // 2) % 2
    c = me % 2
    flips, sends = column_plan()
    planes = range(UNROLL)

    def at(zi, xi, ci):
        return zi * INNER + 2 * xi + ci

    xpeer = at(z, 1 - x, 1 - c)
    cpeer = at(z, x, 1 - c)
    has_prev = me > 0
    has_next = me < count - 1
    prev = jnp.maximum(me - 1, 0)
    after = jnp.minimum(me + 1, count - 1)
    down_plane = (x == 0) & (c == 0) & (z > 0)
    up_plane = (x == 1) & (c == 1) & (z < UNROLL - 1)

    def flagged(values):
        chosen = among(z, [int(v) for v in values])
        return bool(chosen) if isinstance(chosen, int) else chosen == 1

    def signal(sem, device):
        pl.semaphore_signal(sem, inc=1, device_id={"row": device}, device_id_type=MESH)

    def partners(a, b):
        return (a, b) in sends or (b, a) in sends

    barrier = pltpu.get_barrier_semaphore()
    for q in planes:
        @_when(flagged([q > a and partners(a, q) for a in planes]))
        def _():
            signal(barrier, at(q, x, 1 - c))

    @pl.when(x == 0)
    def _():
        signal(barrier, xpeer)

    @pl.when(c == 0)
    def _():
        signal(barrier, cpeer)

    @pl.when(up_plane)
    def _():
        signal(barrier, after)

    own = pl.ds(width, tokens)
    loads = [
        pltpu.make_async_copy(feat_hbm, src.at[own], load_sem.at[0]),
        pltpu.make_async_copy(wq_hbm, wq, load_sem.at[1]),
        pltpu.make_async_copy(wk_hbm, wk, load_sem.at[2]),
        pltpu.make_async_copy(cache_hbm, ext.at[:, own], load_sem.at[3]),
        pltpu.make_async_copy(wv_hbm, wv, load_sem.at[4]),
        pltpu.make_async_copy(wo_hbm, wo, load_sem.at[5]),
        pltpu.make_async_copy(cg_hbm, cg_ref, load_sem.at[6]),
        pltpu.make_async_copy(ng_hbm, ng_ref, load_sem.at[7]),
    ]
    wloads = [pltpu.make_async_copy(cw_hbm.at[t], cw.at[t], cw_sem.at[t]) for t in range(3)]
    loads[0].start()
    loads[7].start()

    lower = among(z, [sum(partners(q, a) for q in range(a)) for a in planes])

    @pl.when(me > 0)
    def _():
        pl.semaphore_wait(barrier, lower + x + c + jnp.where(down_plane, 1, 0))

    for q in planes[:-1]:
        @_when(flagged([q < a and (q, a) in sends for a in planes]))
        def _():
            signal(reply.at[z], at(q, x, 1 - c))

    @pl.when(x == 1)
    def _():
        signal(reply.at[UNROLL], xpeer)

    @pl.when(c == 1)
    def _():
        signal(reply.at[UNROLL + 1], cpeer)

    @pl.when(down_plane)
    def _():
        signal(reply.at[UNROLL + 2], prev)

    for copy in (loads[1], loads[2], loads[4], loads[5], loads[3], wloads[0], wloads[1], loads[6], wloads[2]):
        copy.start()

    def remote(a, b, send, receive, device):
        return pltpu.make_async_remote_copy(
            src_ref=a,
            dst_ref=b,
            send_sem=send,
            recv_sem=receive,
            device_id={"row": device},
            device_id_type=MESH,
        )

    def halo(a, b, index, device):
        return remote(a, b, halo_send.at[index], halo_recv.at[index], device)

    first = pl.ds(0, width)
    last = pl.ds(tokens - width, width)
    low = pl.ds(0, width)
    high = pl.ds(width + tokens, width)
    up_f = halo(feat_hbm.at[last], src.at[low], 0, after)
    down_f = halo(feat_hbm.at[first], src.at[high], 1, prev)
    up_c = halo(cache_hbm.at[:, last], ext.at[:, low], 2, after)
    down_c = halo(cache_hbm.at[:, first], ext.at[:, high], 3, prev)

    def put(ident, device, sem):
        part = blocks.at[ident]
        return remote(part, part, sem, recv.at[ident], device)

    def z_send(j):
        dest = among(z, [DIRECT[a][j] if j < len(DIRECT[a]) else 0 for a in planes])

        @_when(flagged([j < len(DIRECT[a]) for a in planes]))
        def _():
            @pl.when(dest > z)
            def _():
                pl.semaphore_wait(reply.at[dest], 1)

            put(me, at(dest, x, 1 - c), own_send.at[j]).start()

    def x_own():
        @pl.when(x == 0)
        def _():
            pl.semaphore_wait(reply.at[UNROLL], 1)

        put(me, xpeer, own_send.at[3]).start()

    def arrived(ident):
        put(ident, cpeer, own_send.at[0]).wait_recv()

    @pl.when(has_prev)
    def _():
        down_f.start()

    loads[0].wait()
    loads[7].wait()
    gain = ng_ref[...].reshape(1, channels)
    blocks[me] = _rms(src[own, :].astype(F32), gain).astype(BF16)
    z_send(0)
    x_own()
    z_send(1)

    @pl.when(c == 0)
    def _():
        pl.semaphore_wait(reply.at[UNROLL + 1], 1)

    @pl.when(up_plane)
    def _():
        pl.semaphore_wait(reply.at[UNROLL + 2], 1)

    @pl.when(has_next)
    def _():
        up_f.start()


    @pl.when(has_next)
    def _():
        up_c.start()

    @pl.when(has_prev)
    def _():
        down_c.start()

    z_send(2)

    zero = jnp.zeros((width, channels), BF16)

    @pl.when(jnp.logical_not(has_prev))
    def _():
        src[low, :] = zero
        for t in range(ext.shape[0]):
            ext[t, low, :] = zero

    @pl.when(jnp.logical_not(has_next))
    def _():
        src[high, :] = zero
        for t in range(ext.shape[0]):
            ext[t, high, :] = zero

    def conv(frame, t):
        taps = jnp.concatenate(
            [frame[dy * width : dy * width + tokens] for dy in range(3)], axis=-1
        )
        sums = []
        for dx in range(3):
            part = jnp.dot(
                taps,
                cw[t, :, dx].reshape(3 * channels, channels),
                preferred_element_type=F32,
            )
            if t == 0:
                cacc[dx] = part
            elif t == 1:
                cacc[dx] += part
            else:
                sums.append(cacc[dx] + part)
        return sums

    def attend(idents, rows=slice(None), opening=False):
        keys = jnp.concatenate([blocks[u] for u in idents], axis=0)
        scores = lax.dot_general(
            qs[rows, :], keys, (((1,), (1,)), ((), ())), preferred_element_type=F32
        )
        peak = jnp.max(scores, axis=-1, keepdims=True)
        if opening:
            new = peak
        else:
            old = m_ref[rows, :]
            new = jnp.maximum(old, peak)
            scale = jnp.exp2(old - new)
        expw = jnp.exp2(scores - new)
        m_ref[rows, :] = new
        mass = jnp.sum(expw, axis=-1, keepdims=True)
        value = jnp.dot(expw.astype(BF16), keys, preferred_element_type=F32)
        if opening:
            l_ref[rows, :] = mass
            acc[rows, :] = value
        else:
            l_ref[rows, :] = l_ref[rows, :] * scale + mass
            acc[rows, :] = acc[rows, :] * scale + value

    def column(j):
        q = among(z, [ARRIVE[a][j] for a in planes])
        flip = among(z, [flips[a, ARRIVE[a][j]] for a in planes])
        return q, c + flip - 2 * c * flip

    def stage_z(j):
        q, core = column(j)
        ident = at(q, x, core)
        arrived(ident)
        if any(RELAY.values()):
            relayed = among(z, [RELAY[a][0][0] if RELAY[a] else UNROLL for a in planes])
            dest = among(z, [RELAY[a][0][1] if RELAY[a] else 0 for a in planes])

            @pl.when(q == relayed)
            def _():
                put(ident, at(dest, x, 1 - c), relay_send.at[0]).start()

        @_when(flagged([ARRIVE[a][j] != SIDE[a] for a in planes]))
        def _():
            put(ident, xpeer, x_send.at[j]).start()

        return ident

    def stage_side():
        arrived(xpeer)
        for step in (-1, 1):
            @_when(flagged([SIDE.get(a + step) == a for a in planes]))
            def _():
                put(xpeer, at(z + step, x, 1 - c), side_send.at[(step + 1) // 2]).start()

    def stage_x(j):
        q, core = column(j)
        ident = at(q, 1 - x, 1 - core)
        arrived(ident)
        return ident

    def stage_late(j):
        ident = stage_x(j)
        put(ident, cpeer, late_send.at[j]).start()
        return ident

    def stage_peer(j):
        q, core = column(j)
        ident = at(q, 1 - x, core)
        arrived(ident)
        return ident

    loads[4].wait()
    loads[5].wait()
    wvo[...] = jnp.dot(wv[...], wo[...], preferred_element_type=F32).astype(BF16)
    z0 = stage_z(0)
    stage_side()
    z1 = stage_z(1)
    @pl.when(has_prev)
    def _():
        up_f.wait_recv()

    @pl.when(has_next)
    def _():
        down_f.wait_recv()

    loads[1].wait()
    loads[2].wait()
    mine = pl.ds(pl.multiple_of(c * half, 16), half)
    rows = src[pl.ds(pl.multiple_of(c * width, 16), half), :].astype(F32)
    query = jnp.dot(_rms(rows, gain).astype(BF16), wq[...], preferred_element_type=F32).astype(BF16)
    folded = lax.dot_general(
        query, wk[...], (((1,), (1,)), ((), ())), preferred_element_type=F32
    )
    qs[mine, :] = (folded * (channels**-0.5 * math.log2(math.e))).astype(BF16)
    share = remote(qs.at[mine], qs.at[mine], pair_send.at[0], pair_recv.at[0], cpeer)
    share.start()
    z2 = stage_z(2)
    share.wait_recv()
    attend([me, xpeer, z0, z1], opening=True)
    loads[3].wait()

    @pl.when(has_prev)
    def _():
        up_c.wait_recv()

    @pl.when(has_next)
    def _():
        down_c.wait_recv()

    wloads[0].wait()
    conv(ext[0], 0)
    x0 = stage_x(0)
    attend([z2, x0])
    theirs = pl.ds(pl.multiple_of((1 - c) * tokens, 16), total)
    window = pl.ds(pl.multiple_of(c * tokens, 16), total)
    part_acc[...] = acc[theirs, :].astype(BF16)
    lane = lax.broadcasted_iota(jnp.int32, part_ml.shape, 1)
    part_ml[...] = jnp.where(lane < part_ml.shape[1] // 2, m_ref[theirs, :], l_ref[theirs, :])
    give = [
        remote(part_acc, peer_acc, pair_send.at[1], pair_recv.at[1], cpeer),
        remote(part_ml, peer_ml, pair_send.at[2], pair_recv.at[2], cpeer),
    ]
    for copy in give:
        copy.start()

    def merge():
        for copy in give:
            copy.wait_recv()
        peer_m = peer_ml[:, :1]
        peer_l = peer_ml[:, part_ml.shape[1] // 2 :][:, :1]
        own_m = m_ref[window, :]
        new = jnp.maximum(own_m, peer_m)
        own_w = jnp.exp2(own_m - new)
        peer_w = jnp.exp2(peer_m - new)
        m_ref[window, :] = new
        l_ref[window, :] = l_ref[window, :] * own_w + peer_l * peer_w
        acc[window, :] = acc[window, :] * own_w + peer_acc[...].astype(F32) * peer_w

    wloads[1].wait()
    conv(ext[1], 1)
    x1 = stage_late(1)
    x2 = stage_late(2)
    merge()
    attend([x1, x2], window)
    for j in range(3):
        @_when(flagged([j < len(DIRECT[a]) for a in planes]))
        def _():
            put(me, cpeer, own_send.at[j]).wait_send()

        @_when(flagged([ARRIVE[a][j] != SIDE[a] for a in planes]))
        def _():
            put(me, cpeer, x_send.at[j]).wait_send()

    for step in (-1, 1):
        @_when(flagged([SIDE.get(a + step) == a for a in planes]))
        def _():
            put(me, cpeer, side_send.at[(step + 1) // 2]).wait_send()

    put(me, cpeer, own_send.at[3]).wait_send()

    @_when(flagged([bool(RELAY[a]) for a in planes]))
    def _():
        put(me, cpeer, relay_send.at[0]).wait_send()

    @pl.when(has_next)
    def _():
        up_f.wait_send()
        up_c.wait_send()

    @pl.when(has_prev)
    def _():
        down_f.wait_send()
        down_c.wait_send()

    share.wait_send()
    for copy in give:
        copy.wait_send()
    loads[6].wait()
    wloads[2].wait()

    attend([stage_peer(1), stage_peer(2)], window)
    for j in (1, 2):
        put(me, cpeer, late_send.at[j]).wait_send()
    mixed = acc[window, :] * (1.0 / l_ref[window, :])
    residual = src[...].astype(F32) + jnp.dot(
        mixed.astype(BF16), wvo[...], preferred_element_type=F32
    )
    res_ref[...] = residual[width : width + tokens]
    v = _rms(residual, cg_ref[...].reshape(1, channels))
    activated = 0.5 * v * (1.0 + jnp.tanh(0.5 * v))
    spot = lax.broadcasted_iota(jnp.int32, (total, 1), 0)
    start = jnp.where(has_prev, 0, width)
    stop = jnp.where(has_next, total, total - width)
    activated = jnp.where((spot >= start) & (spot < stop), activated, 0.0).astype(BF16)
    sums = conv(activated, 2)
    column_of = lax.broadcasted_iota(jnp.int32, (tokens, 1), 0) % width
    left = jnp.where(column_of == 0, 0.0, pltpu.roll(sums[0], 1, 0))
    right = jnp.where(column_of == width - 1, 0.0, pltpu.roll(sums[2], tokens - 1, 0))
    out_ref[...] = (left + sums[1] + right).astype(BF16)


def settle(residual, conv_out, residual_hbm, out_hbm, sem):
    copies = [
        pltpu.make_async_copy(residual, residual_hbm, sem.at[0]),
        pltpu.make_async_copy(conv_out, out_hbm, sem.at[1]),
    ]
    for copy in copies:
        copy.start()
    for copy in copies:
        copy.wait()


def shards(features, conv_cache, norm_gain, w_query, w_key, w_value, w_out, conv_gain, conv_weight):
    frames, rows, width, channels = features.shape
    cached = conv_cache.shape[0]
    tokens = rows * width
    total = tokens + 2 * width
    count = lax.axis_size("row")
    outer = count // INNER
    hbm = pl.BlockSpec(memory_space=pltpu.HBM)
    vmem = pl.BlockSpec(memory_space=pltpu.VMEM)
    dma = pltpu.SemaphoreType.DMA
    square = pltpu.VMEM((channels, channels), BF16)
    lead = [pltpu.VMEM((channels,), F32), pltpu.VMEM((channels,), F32), pltpu.VMEM((count, tokens, channels), BF16)]
    lead += [pltpu.VMEM((total, channels), BF16), pltpu.VMEM((cached, total, channels), BF16)]
    lead += [square, square, square, square]
    kernels = pltpu.VMEM(conv_weight.shape, BF16)
    summed = pltpu.VMEM((3, tokens, channels), F32)
    if outer == UNROLL:
        body = grid_kernel
        both = 2 * (tokens + width)
        lanes = 128
        scratch = lead + [
            square,
            kernels,
            pltpu.VMEM((both, channels), BF16),
            pltpu.VMEM((both, 1), F32),
            pltpu.VMEM((both, 1), F32),
            pltpu.VMEM((both, channels), F32),
            pltpu.VMEM((total, channels), BF16),
            pltpu.VMEM((total, lanes), F32),
            pltpu.VMEM((total, channels), BF16),
            pltpu.VMEM((total, lanes), F32),
            summed,
            dma((8,)),
            dma((3,)),
            dma((4,)),
            dma((4,)),
            dma((4,)),
            dma((1,)),
            dma((3,)),
            dma((2,)),
            dma((3,)),
            dma((count,)),
            dma((3,)),
            dma((3,)),
            pltpu.SemaphoreType.REGULAR((UNROLL + 3,)),
        ]
    else:
        body = ring
        scratch = lead + [
            kernels,
            pltpu.VMEM((total, channels), BF16),
            pltpu.VMEM((total, 1), F32),
            pltpu.VMEM((total, 1), F32),
            pltpu.VMEM((total, channels), F32),
            summed,
            dma((8,)),
            dma((3,)),
            dma((4,)),
            dma((4,)),
            dma((outer, HALVES)),
            dma((outer, HALVES)),
            dma((2, outer, HALVES)),
            dma((count, HALVES)),
        ]
    residual, conv_out = pl.pallas_call(
        functools.partial(body, count, width),
        out_shape=(
            jax.ShapeDtypeStruct((tokens, channels), F32),
            jax.ShapeDtypeStruct((tokens, channels), BF16),
        ),
        in_specs=[hbm] * 9,
        out_specs=(vmem, vmem),
        scratch_shapes=scratch,
        compiler_params=pltpu.CompilerParams(
            collective_id=0, has_side_effects=True, vmem_limit_bytes=48 << 20
        ),
    )(
        *(
            pltpu.with_memory_space_constraint(x, pltpu.HBM)
            for x in (
                features.reshape(tokens, channels),
                conv_cache.reshape(cached, tokens, channels),
                norm_gain,
                w_query,
                w_key,
                w_value,
                w_out,
                conv_gain,
                conv_weight,
            )
        )
    )
    residual, conv_out = pl.pallas_call(
        settle,
        out_shape=(
            jax.ShapeDtypeStruct((tokens, channels), F32),
            jax.ShapeDtypeStruct((tokens, channels), BF16),
        ),
        in_specs=[vmem, vmem],
        out_specs=(hbm, hbm),
        scratch_shapes=[dma((2,))],
    )(*(pltpu.with_memory_space_constraint(a, pltpu.VMEM) for a in (residual, conv_out)))
    return (
        residual.reshape(frames, rows, width, channels),
        conv_out.reshape(frames, rows, width, channels),
    )


def solution(mesh):
    placed = (
        P(None, ("clip", "row"), None, None),
        P(None, ("clip", "row"), None, None),
        P(),
        P(),
        P(),
        P(),
        P(),
        P(),
        P(),
    )
    return jax.shard_map(
        shards,
        mesh=mesh,
        in_specs=placed,
        out_specs=(P(None, ("clip", "row"), None, None), P(None, ("clip", "row"), None, None)),
        check_vma=False,
    )
```
